32 devices in a mesh: section: 8 (over z, x), dp: 4 (over y, core).
Axes of the slice: x: 2, y: 2, z: 4, core: 2. Of those that a mesh axis runs over, the one named last changes fastest.
Arguments:
- block_arguments: bfloat16 [2, 4, 1024, 2048], P(None, 'dp', 'section'), may hold values from -6 to 6
- incoming_batches: bfloat16 [2, 4, 128, 2048], P(None, 'dp'), may hold values from -6 to 6
- output_adjoints: bfloat16 [2, 4, 1024, 2048], P(None, 'dp', 'section'), may hold values from -0.125 to 0.125
- objective_adjoints: bfloat16 [2, 4, 128, 2048], P(None, 'dp'), may hold values from -0.125 to 0.125
- kept_block_arguments: bfloat16 [2, 2, 4, 1024, 2048], P(None, None, 'dp', 'section'), may hold values from -6 to 6
- parameter_arrays: bfloat16 [8, 2048, 1536], P('section', 'dp'), may hold values from -0.125 to 0.125
Outputs:
- ahead_out: bfloat16 [2, 4, 1024, 2048], P(None, 'dp', 'section')
- section_grads: float32 [8, 2048, 1536], P('section', 'dp')
The draws below stay inside these ranges and needn't reach their ends.
All inputs are finite; a program needn't handle non-finite values.
Results may differ from the reference program's by a relative error of at most 0.013.
Values may be sent and summed in bfloat16 or wider, within the bound.
A program may use at most 128 MiB of HBM per device.

```python
import jax
import jax.numpy as jnp
from jax import lax

HIDDEN_FEATURES = 2048
FF = 512
SMALL_BATCH_SPAN = 128
GRAD_ROWS = 2048
N_SECTION = 8
N_DP = 4


def block_scale(rng, dims, pieces, low, largest):
    level, own = 1.0, jax.random.fold_in(rng, 6)
    for dim, parts in pieces:
        steps = jnp.exp(jax.random.uniform(jax.random.fold_in(own, dim), (parts,), jnp.float32, low / len(pieces), largest / len(pieces)))
        level = level * jnp.repeat(steps, dims[dim] // parts).reshape([-1 if axis == dim else 1 for axis in range(len(dims))])
    return level


def gaussian(stream_key, extent, width, limit, shards=(), held_as=jnp.bfloat16):
    drawn = width * jax.random.normal(stream_key, extent, jnp.float32)
    if shards:
        drawn = drawn * block_scale(stream_key, extent, shards, -0.22, 0.18)
    return jnp.clip(drawn, -limit, limit).astype(held_as)


def setup_inputs(seed: int = 0) -> dict:
    arg_keys = jax.random.split(jax.random.key(seed), 7)
    block_arguments = gaussian(arg_keys[0], (2, N_DP, N_SECTION * SMALL_BATCH_SPAN, HIDDEN_FEATURES), 1.0, 6.0, ((1, 4), (2, 8)))
    incoming_batches = gaussian(arg_keys[1], (2, N_DP, SMALL_BATCH_SPAN, HIDDEN_FEATURES), 1.0, 6.0, ((1, 4),))
    output_adjoints = gaussian(arg_keys[2], (2, N_DP, N_SECTION * SMALL_BATCH_SPAN, HIDDEN_FEATURES), (1.0 / GRAD_ROWS ** 0.5), 0.125, ((1, 4), (2, 8)))
    objective_adjoints = gaussian(arg_keys[3], (2, N_DP, SMALL_BATCH_SPAN, HIDDEN_FEATURES), (1.0 / GRAD_ROWS ** 0.5), 0.125, ((1, 4),))
    kept_block_arguments = gaussian(arg_keys[4], (2, 2, N_DP, N_SECTION * SMALL_BATCH_SPAN, HIDDEN_FEATURES), 1.0, 6.0, ((2, 4), (3, 8)))
    parameter_arrays = gaussian(arg_keys[5], (N_SECTION, HIDDEN_FEATURES, 3 * FF), HIDDEN_FEATURES ** -0.5, 0.125, ((0, 8), (1, 4)))
    return {"block_arguments": block_arguments, "incoming_batches": incoming_batches, "output_adjoints": output_adjoints, "objective_adjoints": objective_adjoints, "kept_block_arguments": kept_block_arguments, "parameter_arrays": parameter_arrays}


def normalize(row_block):
    values = row_block.astype(jnp.float32)
    inverse = lax.rsqrt(lax.optimization_barrier(jnp.mean(values * values, axis=-1, keepdims=True)) + 1e-06)
    return (values, inverse, (values * inverse).astype(jnp.bfloat16))

def section_forward(row_block, matrix):
    hidden_width = matrix.shape[1] // 3
    values, inverse, normed = normalize(row_block)
    projected = jnp.dot(normed, matrix[:, :2 * hidden_width], preferred_element_type=jnp.float32)
    gate_part = projected[:, :hidden_width]
    up_part = projected[:, hidden_width:]
    hidden = (gate_part * jax.nn.sigmoid(gate_part) * up_part).astype(jnp.bfloat16)
    branch = lax.dot_general(hidden, matrix[:, 2 * hidden_width:], (((1,), (1,)), ((), ())), preferred_element_type=jnp.float32)
    return (values + branch).astype(jnp.bfloat16)

def section_reverse_pass(row_block, cotangent, matrix, with_input):
    hidden_width = matrix.shape[1] // 3
    values, inverse, normed = normalize(row_block)
    projected = jnp.dot(normed, matrix[:, :2 * hidden_width], preferred_element_type=jnp.float32)
    gate_part = projected[:, :hidden_width]
    up_part = projected[:, hidden_width:]
    sigmoid_gate = jax.nn.sigmoid(gate_part)
    silu_gate = gate_part * sigmoid_gate
    hidden = (silu_gate * up_part).astype(jnp.bfloat16)
    hidden_grad = jnp.dot(cotangent, matrix[:, 2 * hidden_width:], preferred_element_type=jnp.float32)
    projected_grad = jnp.concatenate([hidden_grad * up_part * sigmoid_gate * (1.0 + gate_part * (1.0 - sigmoid_gate)), hidden_grad * silu_gate], axis=1).astype(jnp.bfloat16)
    inward_grad = lax.dot_general(normed, projected_grad, (((0,), (0,)), ((), ())), preferred_element_type=jnp.float32)
    outward_grad = lax.dot_general(cotangent, hidden, (((0,), (0,)), ((), ())), preferred_element_type=jnp.float32)
    weight_term = jnp.concatenate([inward_grad, outward_grad], axis=1)
    if not with_input:
        return (weight_term, None)
    normed_grad = lax.dot_general(projected_grad, matrix[:, :2 * hidden_width], (((1,), (1,)), ((), ())), preferred_element_type=jnp.float32)
    inner_sum = lax.optimization_barrier(jnp.mean(normed_grad * values, axis=-1, keepdims=True))
    input_grad = cotangent.astype(jnp.float32) + inverse * normed_grad - values * inverse * inverse * inverse * inner_sum
    return (weight_term, input_grad.astype(jnp.bfloat16))

def replica_sums(first_rows, first_cot, second_rows, second_cot, matrix):

    def add_one(total, items):
        rows_one, cot_one, rows_two, cot_two = items
        term_one, discarded_value = section_reverse_pass(rows_one, cot_one, matrix, False)
        term_two, discarded_second = section_reverse_pass(rows_two, cot_two, matrix, False)
        rounded = lax.optimization_barrier((term_one + term_two).astype(jnp.bfloat16))
        return (total + rounded.astype(jnp.float32), None)
    start = jnp.zeros((HIDDEN_FEATURES, 3 * FF), jnp.float32)
    total, discarded_value = lax.scan(add_one, start, (first_rows, first_cot, second_rows, second_cot))
    return total

def reference(block_arguments, incoming_batches, output_adjoints, objective_adjoints, kept_block_arguments, parameter_arrays):
    segment_sequence_catalog = N_SECTION
    first_in = block_arguments.reshape(2, N_DP, segment_sequence_catalog, SMALL_BATCH_SPAN, HIDDEN_FEATURES)
    first_cot = output_adjoints.reshape(2, N_DP, segment_sequence_catalog, SMALL_BATCH_SPAN, HIDDEN_FEATURES)
    retained_intermediates = kept_block_arguments.reshape(2, 2, N_DP, segment_sequence_catalog, SMALL_BATCH_SPAN, HIDDEN_FEATURES)
    matrices = jnp.stack([parameter_arrays, parameter_arrays[::-1]])

    def flatten_rows(rows):
        return rows.reshape(N_DP * SMALL_BATCH_SPAN, HIDDEN_FEATURES)

    def shaped(rows):
        return rows.reshape(N_DP, SMALL_BATCH_SPAN, HIDDEN_FEATURES)

    def first_pass(position):
        forward_list = []
        back_list = []
        for course in range(2):
            matrix = matrices[course, position]
            forward_list.append(shaped(section_forward(flatten_rows(first_in[course, :, position]), matrix)))
            discarded_value, back_rows = section_reverse_pass(flatten_rows(retained_intermediates[course, 0, :, position]), flatten_rows(first_cot[course, :, position]), matrix, True)
            back_list.append(shaped(back_rows))
        return (jnp.stack(forward_list), jnp.stack(back_list))
    first_out, returned = lax.map(first_pass, jnp.arange(segment_sequence_catalog))
    down_in = jnp.concatenate([incoming_batches[0][None], first_out[:-1, 0]], axis=0)
    up_in = jnp.concatenate([first_out[1:, 1], incoming_batches[1][None]], axis=0)
    descending_adjoint = jnp.concatenate([returned[1:, 0], objective_adjoints[0][None]], axis=0)
    ascending_adjoint = jnp.concatenate([objective_adjoints[1][None], returned[:-1, 1]], axis=0)
    second_in = jnp.stack([down_in, up_in], axis=1)
    second_cot = jnp.stack([descending_adjoint, ascending_adjoint], axis=1)

    def second_pass(position):
        forward_list = []
        sum_list = []
        for course in range(2):
            matrix = matrices[course, position]
            forward_list.append(shaped(section_forward(flatten_rows(second_in[position, course]), matrix)))
            sum_list.append(replica_sums(retained_intermediates[course, 0, :, position], first_cot[course, :, position], retained_intermediates[course, 1, :, position], second_cot[position, course], matrix))
        return (jnp.stack(forward_list), jnp.stack(sum_list))
    later_out, totals = lax.map(second_pass, jnp.arange(segment_sequence_catalog))
    section_grads = totals[:, 0] + totals[::-1, 1]
    ahead_out = jnp.transpose(later_out, (1, 2, 0, 3, 4)).reshape(2, N_DP, segment_sequence_catalog * SMALL_BATCH_SPAN, HIDDEN_FEATURES)
    return (ahead_out, section_grads)
```

```python
import functools

import jax
import jax.numpy as jnp
from jax import lax
from jax.experimental import pallas as pl
from jax.experimental.pallas import tpu as pltpu
from jax.sharding import PartitionSpec as P

MESH = pl.DeviceIdType.MESH
BF = jnp.bfloat16
F32 = jnp.float32
TILE = 256
CHUNK = 128
NT = (((1,), (1,)), ((), ()))
TN = (((0,), (0,)), ((), ()))


def normalize_into(src, dst):
    values = src[...].astype(F32)
    inverse = lax.rsqrt(jnp.mean(values * values, axis=-1, keepdims=True) + 1e-06)
    dst[...] = (values * inverse).astype(BF)
    return inverse


def tiles(count, body):
    def step(j, carry):
        body(pl.multiple_of(j * TILE, TILE))
        return carry

    lax.fori_loop(0, count // TILE, step, 0)


def forward(rows, out, weights, normed, hidden):
    width = weights.shape[1] // 3
    normalize_into(rows, normed)

    def hidden_tile(at):
        gate = jnp.dot(normed[...], weights[:, pl.ds(at, TILE)], preferred_element_type=F32)
        up = jnp.dot(normed[...], weights[:, pl.ds(width + at, TILE)], preferred_element_type=F32)
        hidden[:, pl.ds(at, TILE)] = (gate * jax.nn.sigmoid(gate) * up).astype(BF)

    tiles(width, hidden_tile)

    def out_tile(at):
        branch = lax.dot_general(
            hidden[...], weights[pl.ds(at, TILE), 2 * width :], NT, preferred_element_type=F32
        )
        out[:, pl.ds(at, TILE)] = (rows[:, pl.ds(at, TILE)].astype(F32) + branch).astype(BF)

    tiles(weights.shape[0], out_tile)


def backward(rows, cotangent, weights, normed, hidden, pre_grad, back, scratch):
    width = weights.shape[1] // 3
    inverse = normalize_into(rows, normed)

    def hidden_tile(at):
        gate = jnp.dot(normed[...], weights[:, pl.ds(at, TILE)], preferred_element_type=F32)
        up = jnp.dot(normed[...], weights[:, pl.ds(width + at, TILE)], preferred_element_type=F32)
        grad = jnp.dot(
            cotangent[...], weights[:, pl.ds(2 * width + at, TILE)], preferred_element_type=F32
        )
        sig = jax.nn.sigmoid(gate)
        silu = gate * sig
        hidden[:, pl.ds(at, TILE)] = (silu * up).astype(BF)
        pre_grad[:, pl.ds(at, TILE)] = (grad * up * sig * (1.0 + gate * (1.0 - sig))).astype(BF)
        pre_grad[:, pl.ds(width + at, TILE)] = (grad * silu).astype(BF)

    tiles(width, hidden_tile)
    if back is None:
        return

    def grad_tile(at):
        scratch[:, pl.ds(at, TILE)] = lax.dot_general(
            pre_grad[...], weights[pl.ds(at, TILE), : 2 * width], NT, preferred_element_type=F32
        )

    tiles(weights.shape[0], grad_tile)
    values = rows[...].astype(F32)
    grad = scratch[...]
    inner = jnp.mean(grad * values, axis=-1, keepdims=True)
    back[...] = (
        cotangent[...].astype(F32)
        + inverse * grad
        - values * (inverse * inverse * inverse * inner)
    ).astype(BF)


def kernel(
    sections, replicas,
    x_hbm, inc_hbm, cot_hbm, obj_hbm, kept_hbm, w_hbm,
    out_hbm, grads_hbm,
    weights, x1, x2, kept, cots, normed, pre_grad, hidden, fo, fb, out2,
    fwd_normed, fwd_hidden, scratch,
    part_send, part_recv, keep, sum_send, sum_recv, total,
    lsem, wsem_s, wsem_r, psem_s, psem_r, msem_s, msem_r, rsem_s, rsem_r, gsem_s, gsem_r, ysem_s, ysem_r,
):
    s = lax.axis_index("section")
    d = lax.axis_index("dp")
    span = x1.shape[0] // 2
    shard = w_hbm.shape[1]
    groups = replicas // 2
    g, c = d // 2, lax.rem(d, 2)
    partner = (s, g * 2 + 1 - c)
    mirror = (sections - 1 - s, d)
    not_first = s > 0
    not_last = s < sections - 1
    peers = [(s, lax.rem(g + t, groups) * 2 + c) for t in range(1, groups)]
    senders = [lax.rem(g - t + groups, groups) for t in range(1, groups)]

    def remote(src, dst, ss, rs, to):
        return pltpu.make_async_remote_copy(
            src_ref=src, dst_ref=dst, send_sem=ss, recv_sem=rs, device_id=to, device_id_type=MESH
        )

    low, high = pl.ds(0, span), pl.ds(span, span)
    half = [pl.ds(i * span, span) for i in range(4)]

    local = [
        (w_hbm.at[0], weights.at[pl.ds(pl.multiple_of(d * shard, shard), shard)]),
        (cot_hbm.at[0, 0], cots.at[half[0]]),
        (kept_hbm.at[0, 0, 0], kept.at[half[0]]),
        (x_hbm.at[0, 0], x1.at[low]),
        (kept_hbm.at[0, 1, 0], kept.at[half[2]]),
    ]
    local = [pltpu.make_async_copy(a, b, lsem.at[i]) for i, (a, b) in enumerate(local)]
    for copy in local:
        copy.start()
    edge_in = [pltpu.make_async_copy(inc_hbm.at[i, 0], x2.at[half[i]], lsem.at[5 + i]) for i in range(2)]
    edge_cot = [
        pltpu.make_async_copy(obj_hbm.at[i, 0], cots.at[half[2 + i]], lsem.at[7 + i]) for i in range(2)
    ]

    @pl.when(s == 0)
    def _():
        for copy in edge_in:
            copy.start()

    @pl.when(s == sections - 1)
    def _():
        for copy in edge_cot:
            copy.start()

    following = (lax.rem(s + 1, sections), d)
    preceding = (lax.rem(s + sections - 1, sections), d)
    greeted = [mirror, partner, following, preceding] + peers
    barrier = pltpu.get_barrier_semaphore()
    for to in greeted:
        pl.semaphore_signal(barrier, inc=1, device_id=to, device_id_type=MESH)
    pl.semaphore_wait(barrier, len(greeted))

    pieces = 2
    piece = shard // pieces

    def w_rows(owner, h):
        return weights.at[pl.ds(pl.multiple_of(owner * shard + h * piece, piece), piece)]

    w_out = [
        [remote(w_hbm.at[0, pl.ds(h * piece, piece)], w_rows(d, h), wsem_s.at[t, h], wsem_r.at[t, h], to) for h in range(pieces)]
        for t, to in enumerate(peers)
    ]
    for h in range(pieces):
        for row in w_out:
            row[h].start()

    def mirrored(src, dst, i):
        return remote(src, dst, msem_s.at[i], msem_r.at[i], mirror)

    m_cot = mirrored(cot_hbm.at[1, 0], cots.at[half[1]], 0)
    m_kept = mirrored(kept_hbm.at[1, 0, 0], kept.at[half[1]], 1)
    m_x = mirrored(x_hbm.at[1, 0], x1.at[high], 2)
    m_kept2 = mirrored(kept_hbm.at[1, 1, 0], kept.at[half[3]], 3)
    m_out = mirrored(out2.at[high], out_hbm.at[1, 0], 4)
    m_cot.start()
    m_kept.start()
    m_x.start()

    p_own = [remote(w_hbm.at[0, pl.ds(h * piece, piece)], w_rows(d, h), psem_s.at[0, h], psem_r.at[0, h], partner) for h in range(pieces)]
    for copy in p_own:
        copy.start()
    p_fwd = [
        [
            remote(w_rows(from_g * 2 + c, h), w_rows(from_g * 2 + c, h), psem_s.at[1 + t, h], psem_r.at[1 + t, h], partner)
            for h in range(pieces)
        ]
        for t, from_g in enumerate(senders)
    ]
    for h in range(pieces):
        for t in range(len(peers)):
            w_out[t][h].wait_recv()
            p_fwd[t][h].start()
    local[0].wait()
    for copies in [p_own] + p_fwd:
        for copy in copies:
            copy.wait_recv()

    relay_f = [remote(fo.at[half[i]], x2.at[half[i]], rsem_s.at[i], rsem_r.at[i], following) for i in range(2)]
    relay_b = [remote(fb.at[half[i]], cots.at[half[2 + i]], rsem_s.at[2 + i], rsem_r.at[2 + i], preceding) for i in range(2)]

    def back_first(i):
        r = half[i]
        backward(kept.at[r], cots.at[r], weights, normed.at[r], hidden.at[r], pre_grad.at[r], fb.at[r], scratch)

        @pl.when(not_first)
        def _():
            relay_b[i].start()

    def ahead_first(i):
        r = half[i]
        forward(x1.at[r], fo.at[r], weights, fwd_normed, fwd_hidden)

        @pl.when(not_last)
        def _():
            relay_f[i].start()

    def back_second(i):
        @pl.when(not_last)
        def _():
            relay_b[i].wait_recv()

        @pl.when(s == sections - 1)
        def _():
            edge_cot[i].wait()

        r = half[2 + i]
        backward(kept.at[r], cots.at[r], weights, normed.at[r], hidden.at[r], pre_grad.at[r], None, None)

    def ahead_second(i):
        @pl.when(not_first)
        def _():
            relay_f[i].wait_recv()

        @pl.when(s == 0)
        def _():
            edge_in[i].wait()

        forward(x2.at[half[i]], out2.at[half[i]], weights, fwd_normed, fwd_hidden)

    local[1].wait()
    local[2].wait()
    back_first(0)
    local[3].wait()
    ahead_first(0)
    m_cot.wait_recv()
    m_kept.wait_recv()
    back_first(1)
    m_kept2.start()
    m_x.wait_recv()
    ahead_first(1)
    local[4].wait()
    back_second(0)
    ahead_second(0)
    out_own = pltpu.make_async_copy(out2.at[low], out_hbm.at[0, 0], lsem.at[9])
    out_own.start()
    ahead_second(1)
    m_out.start()
    m_kept2.wait_recv()
    back_second(1)

    width = weights.shape[1] // 3
    per = shard // CHUNK

    def term(owner, q, put):
        at = pl.multiple_of(owner * shard + q * CHUNK, CHUNK)
        put(slice(0, 2 * width), lax.dot_general(normed[:, pl.ds(at, CHUNK)], pre_grad[...], TN, preferred_element_type=F32))
        put(slice(2 * width, 3 * width), lax.dot_general(cots[:, pl.ds(at, CHUNK)], hidden[...], TN, preferred_element_type=F32))

    def pair_copy(i):
        return remote(part_send.at[i], part_recv.at[i], gsem_s.at[i], gsem_r.at[i], partner)

    def give(owner_group, i, q):
        def put(columns, value):
            part_send[i, :, columns] = value.astype(BF)

        term(owner_group * 2 + 1 - c, q, put)
        pair_copy(i).start()

    def own_term(owner_group, q, store):
        term(owner_group * 2 + c, q, store)

    def loop(count, body):
        def step(q, carry):
            body(q)
            return carry

        lax.fori_loop(0, count, step, 0)

    def sum_copy(i, to):
        return remote(sum_send.at[i], sum_recv.at[i], ysem_s.at[i], ysem_r.at[i], to)

    for t in range(1, groups):
        to_g = lax.rem(g + t, groups)
        loop(per, lambda q: give(to_g, t * per + q, q))

        def pass_on(q):
            def put(columns, value):
                keep[:, columns] = value

            own_term(to_g, q, put)
            pair_copy(t * per + q).wait_recv()
            i = (t - 1) * per + q
            sum_send[i] = (keep[...] + part_recv[t * per + q].astype(F32)).astype(BF)
            sum_copy(i, peers[t - 1]).start()

        loop(per, pass_on)
    loop(per, lambda q: give(g, q, q))

    def finish(q):
        rows = pl.ds(pl.multiple_of(q * CHUNK, CHUNK), CHUNK)

        def put(columns, value):
            total[rows, columns] = value

        own_term(g, q, put)
        pair_copy(q).wait_recv()
        total[rows] = total[rows] + part_recv[q].astype(F32)

    loop(per, finish)

    def collect(q):
        rows = pl.ds(pl.multiple_of(q * CHUNK, CHUNK), CHUNK)
        value = total[rows]
        for t in range(1, groups):
            i = (t - 1) * per + q
            sum_copy(i, peers[t - 1]).wait_recv()
            value = value + sum_recv[i].astype(F32)
        total[rows] = value
        pltpu.make_async_copy(total.at[rows], grads_hbm.at[0, rows], lsem.at[10]).start()

    loop(per, collect)
    pltpu.make_async_copy(total, grads_hbm.at[0], lsem.at[10]).wait()

    out_own.wait()
    m_out.wait_recv()
    for copy in (m_cot, m_kept, m_x, m_kept2, m_out):
        copy.wait_send()
    for row in w_out + [p_own] + p_fwd:
        for copy in row:
            copy.wait_send()

    @pl.when(not_last)
    def _():
        for copy in relay_f:
            copy.wait_send()

    @pl.when(not_first)
    def _():
        for copy in relay_b:
            copy.wait_send()

    loop(groups * per, lambda i: pair_copy(i).wait_send())
    loop((groups - 1) * per, lambda i: sum_copy(i, peers[0]).wait_send())


def on_device(sections, replicas, x, inc, cot, obj, kept, w):
    span, features = x.shape[2:]
    shard, columns = w.shape[1:]
    width = columns // 3
    groups = replicas // 2
    pairs = groups * (shard // CHUNK)
    sums = max(1, (groups - 1) * (shard // CHUNK))
    dma = pltpu.SemaphoreType.DMA
    v = pltpu.VMEM
    any_space = pl.BlockSpec(memory_space=pl.ANY)
    return pl.pallas_call(
        functools.partial(kernel, sections, replicas),
        out_shape=(
            jax.ShapeDtypeStruct(x.shape, BF),
            jax.ShapeDtypeStruct(w.shape, F32),
        ),
        in_specs=[any_space] * 6,
        out_specs=(any_space, any_space),
        scratch_shapes=[
            v((features, columns), BF),
            v((2 * span, features), BF),
            v((2 * span, features), BF),
            v((4 * span, features), BF),
            v((4 * span, features), BF),
            v((4 * span, features), BF),
            v((4 * span, 2 * width), BF),
            v((4 * span, width), BF),
            v((2 * span, features), BF),
            v((2 * span, features), BF),
            v((2 * span, features), BF),
            v((span, features), BF),
            v((span, width), BF),
            v((span, features), F32),
            v((pairs, CHUNK, columns), BF),
            v((pairs, CHUNK, columns), BF),
            v((CHUNK, columns), F32),
            v((sums, CHUNK, columns), BF),
            v((sums, CHUNK, columns), BF),
            v((shard, columns), F32),
            dma((11,)),
            dma((groups, 2)),
            dma((groups, 2)),
            dma((groups, 2)),
            dma((groups, 2)),
            dma((5,)),
            dma((5,)),
            dma((4,)),
            dma((4,)),
            dma((pairs,)),
            dma((pairs,)),
            dma((sums,)),
            dma((sums,)),
        ],
        compiler_params=pltpu.CompilerParams(
            collective_id=0, has_side_effects=True, vmem_limit_bytes=60 * 2**20
        ),
    )(x, inc, cot, obj, kept, w)


def solution(mesh):
    in_specs = (
        P(None, "dp", "section", None),
        P(None, "dp", None, None),
        P(None, "dp", "section", None),
        P(None, "dp", None, None),
        P(None, None, "dp", "section", None),
        P("section", "dp", None),
    )
    out_specs = (P(None, "dp", "section", None), P("section", "dp", None))
    body = functools.partial(on_device, mesh.shape["section"], mesh.shape["dp"])
    return jax.shard_map(body, mesh=mesh, in_specs=in_specs, out_specs=out_specs, check_vma=False)
```

```python
import functools

import jax
import jax.numpy as jnp
from jax import lax
from jax.experimental import pallas as pl
from jax.experimental.pallas import tpu as pltpu
from jax.sharding import PartitionSpec as P

MESH = pl.DeviceIdType.MESH
BF = jnp.bfloat16
F32 = jnp.float32
TILE = 256
CHUNK = 128
NT = (((1,), (1,)), ((), ()))
TN = (((0,), (0,)), ((), ()))


def normalize_into(src, dst):
    values = src[...].astype(F32)
    inverse = lax.rsqrt(jnp.mean(values * values, axis=-1, keepdims=True) + 1e-06)
    dst[...] = (values * inverse).astype(BF)
    return inverse


def tiles(count, body):
    def step(j, carry):
        body(pl.multiple_of(j * TILE, TILE))
        return carry

    lax.fori_loop(0, count // TILE, step, 0)


def forward(rows, out, weights, normed, hidden):
    width = weights.shape[1] // 3
    normalize_into(rows, normed)

    def hidden_tile(at):
        gate = jnp.dot(normed[...], weights[:, pl.ds(at, TILE)], preferred_element_type=F32)
        up = jnp.dot(normed[...], weights[:, pl.ds(width + at, TILE)], preferred_element_type=F32)
        hidden[:, pl.ds(at, TILE)] = (gate * jax.nn.sigmoid(gate) * up).astype(BF)

    tiles(width, hidden_tile)

    def out_tile(at):
        branch = lax.dot_general(
            hidden[...], weights[pl.ds(at, TILE), 2 * width :], NT, preferred_element_type=F32
        )
        out[:, pl.ds(at, TILE)] = (rows[:, pl.ds(at, TILE)].astype(F32) + branch).astype(BF)

    tiles(weights.shape[0], out_tile)


def backward(rows, cotangent, weights, normed, hidden, pre_grad, back, scratch):
    width = weights.shape[1] // 3
    inverse = normalize_into(rows, normed)

    def hidden_tile(at):
        gate = jnp.dot(normed[...], weights[:, pl.ds(at, TILE)], preferred_element_type=F32)
        up = jnp.dot(normed[...], weights[:, pl.ds(width + at, TILE)], preferred_element_type=F32)
        grad = jnp.dot(
            cotangent[...], weights[:, pl.ds(2 * width + at, TILE)], preferred_element_type=F32
        )
        sig = jax.nn.sigmoid(gate)
        silu = gate * sig
        hidden[:, pl.ds(at, TILE)] = (silu * up).astype(BF)
        pre_grad[:, pl.ds(at, TILE)] = (grad * up * sig * (1.0 + gate * (1.0 - sig))).astype(BF)
        pre_grad[:, pl.ds(width + at, TILE)] = (grad * silu).astype(BF)

    tiles(width, hidden_tile)
    if back is None:
        return

    def grad_tile(at):
        scratch[:, pl.ds(at, TILE)] = lax.dot_general(
            pre_grad[...], weights[pl.ds(at, TILE), : 2 * width], NT, preferred_element_type=F32
        )

    tiles(weights.shape[0], grad_tile)
    values = rows[...].astype(F32)
    grad = scratch[...]
    inner = jnp.mean(grad * values, axis=-1, keepdims=True)
    back[...] = (
        cotangent[...].astype(F32)
        + inverse * grad
        - values * (inverse * inverse * inverse * inner)
    ).astype(BF)


def kernel(
    sections, replicas,
    x_hbm, inc_hbm, cot_hbm, obj_hbm, kept_hbm, w_hbm,
    out_hbm, grads_hbm,
    weights, x1, x2, kept, cots, normed, pre_grad, hidden, fo, fb, out2,
    fwd_normed, fwd_hidden, scratch, via_kept, via_x,
    part_send, part_recv, keep, sum_send, sum_recv, total,
    lsem, wsem_s, wsem_r, psem_s, psem_r, msem_s, msem_r, rsem_s, rsem_r, gsem_s, gsem_r, ysem_s, ysem_r, vsem_s, vsem_r, turn,
):
    s = lax.axis_index("section")
    d = lax.axis_index("dp")
    span = x1.shape[0] // 2
    shard = w_hbm.shape[1]
    groups = replicas // 2
    g, c = d // 2, lax.rem(d, 2)
    partner = (s, g * 2 + 1 - c)
    mirror = (sections - 1 - s, d)
    not_first = s > 0
    not_last = s < sections - 1
    peers = [(s, lax.rem(g + t, groups) * 2 + c) for t in range(1, groups)]
    senders = [lax.rem(g - t + groups, groups) for t in range(1, groups)]

    def remote(src, dst, ss, rs, to):
        return pltpu.make_async_remote_copy(
            src_ref=src, dst_ref=dst, send_sem=ss, recv_sem=rs, device_id=to, device_id_type=MESH
        )

    low, high = pl.ds(0, span), pl.ds(span, span)
    half = [pl.ds(i * span, span) for i in range(4)]

    local = [
        (w_hbm.at[0], weights.at[pl.ds(pl.multiple_of(d * shard, shard), shard)]),
        (cot_hbm.at[0, 0], cots.at[half[0]]),
        (kept_hbm.at[0, 0, 0], kept.at[half[0]]),
        (x_hbm.at[0, 0], x1.at[low]),
        (kept_hbm.at[0, 1, 0], kept.at[half[2]]),
    ]
    local = [pltpu.make_async_copy(a, b, lsem.at[i]) for i, (a, b) in enumerate(local)]
    for copy in local:
        copy.start()
    edge_in = [pltpu.make_async_copy(inc_hbm.at[i, 0], x2.at[half[i]], lsem.at[5 + i]) for i in range(2)]
    edge_cot = [
        pltpu.make_async_copy(obj_hbm.at[i, 0], cots.at[half[2 + i]], lsem.at[7 + i]) for i in range(2)
    ]

    @pl.when(s == 0)
    def _():
        for copy in edge_in:
            copy.start()

    @pl.when(s == sections - 1)
    def _():
        for copy in edge_cot:
            copy.start()

    following = (lax.rem(s + 1, sections), d)
    preceding = (lax.rem(s + sections - 1, sections), d)
    staged = sections == 8
    greeted = [mirror, partner, following, preceding] + peers
    if staged:
        above = s + 2 - 4 * lax.rem(s // 2, 2)
        beside = s + 1 - 2 * lax.rem(s, 2)
        outer = (s < 2) | (s >= sections - 2)
        inner = (s >= 2) & (s < sections - 2)
        middle = (s == sections // 2 - 1) | (s == sections // 2)
        helper = (s == sections // 2 - 2) | (s == sections // 2 + 1)
        direct = (s < sections // 2 - 1) | (s > sections // 2)
        greeted += [(above, d), (sections - 1 - above, d), (sections - 1 - beside, d)]
    barrier = pltpu.get_barrier_semaphore()
    for to in greeted:
        pl.semaphore_signal(barrier, inc=1, device_id=to, device_id_type=MESH)
    pl.semaphore_wait(barrier, len(greeted))

    pieces = 2
    piece = shard // pieces

    def w_rows(owner, h):
        return weights.at[pl.ds(pl.multiple_of(owner * shard + h * piece, piece), piece)]

    w_out = [
        [remote(w_hbm.at[0, pl.ds(h * piece, piece)], w_rows(d, h), wsem_s.at[t, h], wsem_r.at[t, h], to) for h in range(pieces)]
        for t, to in enumerate(peers)
    ]
    for h in range(pieces):
        for row in w_out:
            row[h].start()

    def mirrored(src, dst, i):
        return remote(src, dst, msem_s.at[i], msem_r.at[i], mirror)

    m_cot = mirrored(cot_hbm.at[1, 0], cots.at[half[1]], 0)
    m_kept = mirrored(kept_hbm.at[1, 0, 0], kept.at[half[1]], 1)
    m_x = mirrored(x_hbm.at[1, 0], x1.at[high], 2)
    m_kept2 = mirrored(kept_hbm.at[1, 1, 0], kept.at[half[3]], 3)
    m_out = mirrored(out2.at[high], out_hbm.at[1, 0], 4)
    m_cot.start()
    m_kept.start()
    if staged:
        k_via = remote(kept_hbm.at[1, 1, 0], via_kept, vsem_s.at[0], vsem_r.at[0], (beside, d))
        x_via = remote(x_hbm.at[1, 0], via_x, vsem_s.at[1], vsem_r.at[1], (above, d))
        k_pass = remote(via_kept, kept.at[half[3]], vsem_s.at[2], msem_r.at[3], (sections - 1 - beside, d))
        x_pass = remote(via_x, x1.at[high], vsem_s.at[3], msem_r.at[2], (sections - 1 - above, d))

        @pl.when(middle)
        def _():
            k_via.start()

        @pl.when(outer & not_first)
        def _():
            x_via.start()

    p_own = [remote(w_hbm.at[0, pl.ds(h * piece, piece)], w_rows(d, h), psem_s.at[0, h], psem_r.at[0, h], partner) for h in range(pieces)]
    for copy in p_own:
        copy.start()
    p_fwd = [
        [
            remote(w_rows(from_g * 2 + c, h), w_rows(from_g * 2 + c, h), psem_s.at[1 + t, h], psem_r.at[1 + t, h], partner)
            for h in range(pieces)
        ]
        for t, from_g in enumerate(senders)
    ]
    for h in range(pieces):
        for t in range(len(peers)):
            w_out[t][h].wait_recv()
            p_fwd[t][h].start()
    local[0].wait()
    for copies in [p_own] + p_fwd:
        for copy in copies:
            copy.wait_recv()

    relay_f = [remote(fo.at[half[i]], x2.at[half[i]], rsem_s.at[i], rsem_r.at[i], following) for i in range(2)]
    relay_b = [remote(fb.at[half[i]], cots.at[half[2 + i]], rsem_s.at[2 + i], rsem_r.at[2 + i], preceding) for i in range(2)]

    def back_first(i):
        r = half[i]
        backward(kept.at[r], cots.at[r], weights, normed.at[r], hidden.at[r], pre_grad.at[r], fb.at[r], scratch)

        @pl.when(not_first)
        def _():
            relay_b[i].start()

    def ahead_first(i, here):
        @pl.when(here & not_last)
        def _():
            if i:
                m_x.wait_recv()
            r = half[i]
            forward(x1.at[r], fo.at[r], weights, fwd_normed, fwd_hidden)
            relay_f[i].start()

    def back_second(i):
        @pl.when(not_last)
        def _():
            relay_b[i].wait_recv()

        @pl.when(s == sections - 1)
        def _():
            edge_cot[i].wait()

        r = half[2 + i]
        backward(kept.at[r], cots.at[r], weights, normed.at[r], hidden.at[r], pre_grad.at[r], None, None)

    def ahead_second(i):
        forward(x2.at[half[i]], out2.at[half[i]], weights, fwd_normed, fwd_hidden)

    def finish_mirrored():
        ahead_second(1)
        if staged:
            pl.when(outer)(lambda: pl.semaphore_wait(turn, 1))
        m_out.start()

    local[1].wait()
    local[2].wait()
    back_first(0)
    if staged:

        pl.when(helper)(m_kept2.start)

        @pl.when(helper)
        def _():
            k_via.wait_recv()
            k_pass.start()
    else:
        m_kept2.start()
    m_cot.wait_recv()
    m_kept.wait_recv()
    back_first(1)
    even = lax.rem(s, 2) == 0
    early = even & (s >= sections // 2)
    soon = even & (s != sections // 2 - 2)
    if staged:
        pl.when(outer)(m_kept2.start)

        @pl.when(inner)
        def _():
            m_x.start()

        @pl.when(inner & (above > 0))
        def _():
            x_via.wait_recv()
            x_pass.start()
    else:
        pl.when(not_first)(m_x.start)
    local[3].wait()
    ahead_first(0, soon)
    local[4].wait()
    back_second(0)
    ahead_first(1, early)
    m_kept2.wait_recv()
    back_second(1)

    width = weights.shape[1] // 3
    per = shard // CHUNK

    def term(owner, q, put):
        at = pl.multiple_of(owner * shard + q * CHUNK, CHUNK)
        put(slice(0, 2 * width), lax.dot_general(normed[:, pl.ds(at, CHUNK)], pre_grad[...], TN, preferred_element_type=F32))
        put(slice(2 * width, 3 * width), lax.dot_general(cots[:, pl.ds(at, CHUNK)], hidden[...], TN, preferred_element_type=F32))

    def pair_copy(i):
        return remote(part_send.at[i], part_recv.at[i], gsem_s.at[i], gsem_r.at[i], partner)

    def give(owner_group, i, q):
        def put(columns, value):
            part_send[i, :, columns] = value.astype(BF)

        term(owner_group * 2 + 1 - c, q, put)
        pair_copy(i).start()

    def own_term(owner_group, q, store):
        term(owner_group * 2 + c, q, store)

    def loop(count, body):
        def step(q, carry):
            body(q)
            return carry

        lax.fori_loop(0, count, step, 0)

    def sum_copy(i, to):
        return remote(sum_send.at[i], sum_recv.at[i], ysem_s.at[i], ysem_r.at[i], to)

    for t in range(1, groups):
        to_g = lax.rem(g + t, groups)
        loop(per, lambda q: give(to_g, t * per + q, q))

        def pass_on(q):
            def put(columns, value):
                keep[:, columns] = value

            own_term(to_g, q, put)
            pair_copy(t * per + q).wait_recv()
            i = (t - 1) * per + q
            sum_send[i] = (keep[...] + part_recv[t * per + q].astype(F32)).astype(BF)
            sum_copy(i, peers[t - 1]).start()

        loop(per, pass_on)

    @pl.when(s == 0)
    def _():
        for copy in edge_in:
            copy.wait()
        finish_mirrored()

    ahead_first(1, jnp.logical_not(early))
    ahead_first(0, jnp.logical_not(soon))
    loop(per, lambda q: give(g, q, q))

    def finish(q):
        rows = pl.ds(pl.multiple_of(q * CHUNK, CHUNK), CHUNK)

        def put(columns, value):
            total[rows, columns] = value

        own_term(g, q, put)
        pair_copy(q).wait_recv()
        total[rows] = total[rows] + part_recv[q].astype(F32)

    loop(per, finish)

    if staged:

        @pl.when(inner)
        def _():
            m_x.wait_send()
            pl.when(above > 0)(x_pass.wait_send)
            pl.semaphore_signal(turn, inc=1, device_id=(above, d), device_id_type=MESH)

    @pl.when(not_first)
    def _():
        relay_f[1].wait_recv()
        finish_mirrored()
        relay_f[0].wait_recv()

    ahead_second(0)
    out_own = pltpu.make_async_copy(out2.at[low], out_hbm.at[0, 0], lsem.at[9])
    out_own.start()

    def collect(q):
        rows = pl.ds(pl.multiple_of(q * CHUNK, CHUNK), CHUNK)
        value = total[rows]
        for t in range(1, groups):
            i = (t - 1) * per + q
            sum_copy(i, peers[t - 1]).wait_recv()
            value = value + sum_recv[i].astype(F32)
        total[rows] = value
        pltpu.make_async_copy(total.at[rows], grads_hbm.at[0, rows], lsem.at[10]).start()

    loop(per, collect)
    pltpu.make_async_copy(total, grads_hbm.at[0], lsem.at[10]).wait()

    out_own.wait()
    m_out.wait_recv()
    for copy in (m_cot, m_kept, m_out):
        copy.wait_send()
    if staged:
        for here, copy in ((direct, m_kept2), (middle, k_via), (outer & not_first, x_via), (helper, k_pass)):
            pl.when(here)(copy.wait_send)
    else:
        m_kept2.wait_send()
        pl.when(not_first)(m_x.wait_send)
    for row in w_out + [p_own] + p_fwd:
        for copy in row:
            copy.wait_send()

    @pl.when(not_last)
    def _():
        for copy in relay_f:
            copy.wait_send()

    @pl.when(not_first)
    def _():
        for copy in relay_b:
            copy.wait_send()

    loop(groups * per, lambda i: pair_copy(i).wait_send())
    loop((groups - 1) * per, lambda i: sum_copy(i, peers[0]).wait_send())


def on_device(sections, replicas, x, inc, cot, obj, kept, w):
    span, features = x.shape[2:]
    shard, columns = w.shape[1:]
    width = columns // 3
    groups = replicas // 2
    pairs = groups * (shard // CHUNK)
    sums = max(1, (groups - 1) * (shard // CHUNK))
    dma = pltpu.SemaphoreType.DMA
    v = pltpu.VMEM
    any_space = pl.BlockSpec(memory_space=pl.ANY)
    return pl.pallas_call(
        functools.partial(kernel, sections, replicas),
        out_shape=(
            jax.ShapeDtypeStruct(x.shape, BF),
            jax.ShapeDtypeStruct(w.shape, F32),
        ),
        in_specs=[any_space] * 6,
        out_specs=(any_space, any_space),
        scratch_shapes=[
            v((features, columns), BF),
            v((2 * span, features), BF),
            v((2 * span, features), BF),
            v((4 * span, features), BF),
            v((4 * span, features), BF),
            v((4 * span, features), BF),
            v((4 * span, 2 * width), BF),
            v((4 * span, width), BF),
            v((2 * span, features), BF),
            v((2 * span, features), BF),
            v((2 * span, features), BF),
            v((span, features), BF),
            v((span, width), BF),
            v((span, features), F32),
            v((span, features), BF),
            v((span, features), BF),
            v((pairs, CHUNK, columns), BF),
            v((pairs, CHUNK, columns), BF),
            v((CHUNK, columns), F32),
            v((sums, CHUNK, columns), BF),
            v((sums, CHUNK, columns), BF),
            v((shard, columns), F32),
            dma((11,)),
            dma((groups, 2)),
            dma((groups, 2)),
            dma((groups, 2)),
            dma((groups, 2)),
            dma((5,)),
            dma((5,)),
            dma((4,)),
            dma((4,)),
            dma((pairs,)),
            dma((pairs,)),
            dma((sums,)),
            dma((sums,)),
            dma((4,)),
            dma((2,)),
            pltpu.SemaphoreType.REGULAR,
        ],
        compiler_params=pltpu.CompilerParams(
            collective_id=0, has_side_effects=True, vmem_limit_bytes=60 * 2**20
        ),
    )(x, inc, cot, obj, kept, w)


def solution(mesh):
    in_specs = (
        P(None, "dp", "section", None),
        P(None, "dp", None, None),
        P(None, "dp", "section", None),
        P(None, "dp", None, None),
        P(None, None, "dp", "section", None),
        P("section", "dp", None),
    )
    out_specs = (P(None, "dp", "section", None), P("section", "dp", None))
    body = functools.partial(on_device, mesh.shape["section"], mesh.shape["dp"])
    return jax.shard_map(body, mesh=mesh, in_specs=in_specs, out_specs=out_specs, check_vma=False)
```

```python
import functools

import jax
import jax.numpy as jnp
from jax import lax
from jax.experimental import pallas as pl
from jax.experimental.pallas import tpu as pltpu
from jax.sharding import PartitionSpec as P

MESH = pl.DeviceIdType.MESH
BF = jnp.bfloat16
F32 = jnp.float32
TILE = 256
CHUNK = 128
NT = (((1,), (1,)), ((), ()))
TN = (((0,), (0,)), ((), ()))


def normalize_into(src, dst):
    values = src[...].astype(F32)
    inverse = lax.rsqrt(jnp.mean(values * values, axis=-1, keepdims=True) + 1e-06)
    dst[...] = (values * inverse).astype(BF)
    return inverse


def tiles(count, body):
    def step(j, carry):
        body(pl.multiple_of(j * TILE, TILE))
        return carry

    lax.fori_loop(0, count // TILE, step, 0)


def forward(rows, out, weights, normed, hidden):
    width = weights.shape[1] // 3
    normalize_into(rows, normed)

    def hidden_tile(at):
        gate = jnp.dot(normed[...], weights[:, pl.ds(at, TILE)], preferred_element_type=F32)
        up = jnp.dot(normed[...], weights[:, pl.ds(width + at, TILE)], preferred_element_type=F32)
        hidden[:, pl.ds(at, TILE)] = (gate * jax.nn.sigmoid(gate) * up).astype(BF)

    tiles(width, hidden_tile)

    def out_tile(at):
        branch = lax.dot_general(
            hidden[...], weights[pl.ds(at, TILE), 2 * width :], NT, preferred_element_type=F32
        )
        out[:, pl.ds(at, TILE)] = (rows[:, pl.ds(at, TILE)].astype(F32) + branch).astype(BF)

    tiles(weights.shape[0], out_tile)


def backward(rows, cotangent, weights, normed, hidden, pre_grad, back, scratch):
    width = weights.shape[1] // 3
    inverse = normalize_into(rows, normed)

    def hidden_tile(at):
        gate = jnp.dot(normed[...], weights[:, pl.ds(at, TILE)], preferred_element_type=F32)
        up = jnp.dot(normed[...], weights[:, pl.ds(width + at, TILE)], preferred_element_type=F32)
        grad = jnp.dot(
            cotangent[...], weights[:, pl.ds(2 * width + at, TILE)], preferred_element_type=F32
        )
        sig = jax.nn.sigmoid(gate)
        silu = gate * sig
        hidden[:, pl.ds(at, TILE)] = (silu * up).astype(BF)
        pre_grad[:, pl.ds(at, TILE)] = (grad * up * sig * (1.0 + gate * (1.0 - sig))).astype(BF)
        pre_grad[:, pl.ds(width + at, TILE)] = (grad * silu).astype(BF)

    tiles(width, hidden_tile)
    if back is None:
        return

    def grad_tile(at):
        scratch[:, pl.ds(at, TILE)] = lax.dot_general(
            pre_grad[...], weights[pl.ds(at, TILE), : 2 * width], NT, preferred_element_type=F32
        )

    tiles(weights.shape[0], grad_tile)
    values = rows[...].astype(F32)
    grad = scratch[...]
    inner = jnp.mean(grad * values, axis=-1, keepdims=True)
    back[...] = (
        cotangent[...].astype(F32)
        + inverse * grad
        - values * (inverse * inverse * inverse * inner)
    ).astype(BF)


def kernel(
    sections, replicas,
    x_hbm, inc_hbm, cot_hbm, obj_hbm, kept_hbm, w_hbm,
    out_hbm, grads_hbm,
    weights, x1, x2, kept, cots, normed, pre_grad, hidden, fo, fb, out2,
    fwd_normed, fwd_hidden, scratch, via_kept, via_x,
    part_send, part_recv, keep, sum_send, sum_recv, total,
    lsem, wsem_s, wsem_r, psem_s, psem_r, msem_s, msem_r, rsem_s, rsem_r, gsem_s, gsem_r, ysem_s, ysem_r, vsem_s, vsem_r, turn, clear,
):
    s = lax.axis_index("section")
    d = lax.axis_index("dp")
    span = x1.shape[0] // 2
    shard = w_hbm.shape[1]
    groups = replicas // 2
    g, c = d // 2, lax.rem(d, 2)
    partner = (s, g * 2 + 1 - c)
    mirror = (sections - 1 - s, d)
    not_first = s > 0
    not_last = s < sections - 1
    peers = [(s, lax.rem(g + t, groups) * 2 + c) for t in range(1, groups)]
    senders = [lax.rem(g - t + groups, groups) for t in range(1, groups)]

    def remote(src, dst, ss, rs, to):
        return pltpu.make_async_remote_copy(
            src_ref=src, dst_ref=dst, send_sem=ss, recv_sem=rs, device_id=to, device_id_type=MESH
        )

    low, high = pl.ds(0, span), pl.ds(span, span)
    half = [pl.ds(i * span, span) for i in range(4)]

    local = [
        (w_hbm.at[0], weights.at[pl.ds(pl.multiple_of(d * shard, shard), shard)]),
        (cot_hbm.at[0, 0], cots.at[half[0]]),
        (kept_hbm.at[0, 0, 0], kept.at[half[0]]),
        (x_hbm.at[0, 0], x1.at[low]),
        (kept_hbm.at[0, 1, 0], kept.at[half[2]]),
    ]
    local = [pltpu.make_async_copy(a, b, lsem.at[i]) for i, (a, b) in enumerate(local)]
    for copy in local:
        copy.start()
    edge_in = [pltpu.make_async_copy(inc_hbm.at[i, 0], x2.at[half[i]], lsem.at[5 + i]) for i in range(2)]
    edge_cot = [
        pltpu.make_async_copy(obj_hbm.at[i, 0], cots.at[half[2 + i]], lsem.at[7 + i]) for i in range(2)
    ]

    @pl.when(s == 0)
    def _():
        for copy in edge_in:
            copy.start()

    @pl.when(s == sections - 1)
    def _():
        for copy in edge_cot:
            copy.start()

    following = (lax.rem(s + 1, sections), d)
    preceding = (lax.rem(s + sections - 1, sections), d)
    staged = sections == 8
    greeted = [mirror, partner, following, preceding] + peers
    if staged:
        above = s + 2 - 4 * lax.rem(s // 2, 2)
        beside = s + 1 - 2 * lax.rem(s, 2)
        outer = (s < 2) | (s >= sections - 2)
        inner = (s >= 2) & (s < sections - 2)
        middle = (s == sections // 2 - 1) | (s == sections // 2)
        helper = (s == sections // 2 - 2) | (s == sections // 2 + 1)
        direct = (s < sections // 2 - 1) | (s > sections // 2)
        greeted += [(above, d), (sections - 1 - above, d), (sections - 1 - beside, d)]
    barrier = pltpu.get_barrier_semaphore()
    for to in greeted:
        pl.semaphore_signal(barrier, inc=1, device_id=to, device_id_type=MESH)
    pl.semaphore_wait(barrier, len(greeted))

    pieces = 2
    piece = shard // pieces

    def w_rows(owner, h):
        return weights.at[pl.ds(pl.multiple_of(owner * shard + h * piece, piece), piece)]

    w_out = [
        [remote(w_hbm.at[0, pl.ds(h * piece, piece)], w_rows(d, h), wsem_s.at[t, h], wsem_r.at[t, h], to) for h in range(pieces)]
        for t, to in enumerate(peers)
    ]
    for h in range(pieces):
        for row in w_out:
            row[h].start()

    def mirrored(src, dst, i):
        return remote(src, dst, msem_s.at[i], msem_r.at[i], mirror)

    m_cot = mirrored(cot_hbm.at[1, 0], cots.at[half[1]], 0)
    m_kept = mirrored(kept_hbm.at[1, 0, 0], kept.at[half[1]], 1)
    m_x = mirrored(x_hbm.at[1, 0], x1.at[high], 2)
    m_kept2 = mirrored(kept_hbm.at[1, 1, 0], kept.at[half[3]], 3)
    m_out = mirrored(out2.at[high], out_hbm.at[1, 0], 4)
    m_cot.start()
    m_kept.start()
    if staged:
        k_via = remote(kept_hbm.at[1, 1, 0], via_kept, vsem_s.at[0], vsem_r.at[0], (beside, d))
        x_via = remote(x_hbm.at[1, 0], via_x, vsem_s.at[1], vsem_r.at[1], (above, d))
        k_pass = remote(via_kept, kept.at[half[3]], vsem_s.at[2], msem_r.at[3], (sections - 1 - beside, d))
        x_pass = remote(via_x, x1.at[high], vsem_s.at[3], msem_r.at[2], (sections - 1 - above, d))

        @pl.when(middle)
        def _():
            k_via.start()

        @pl.when(outer & not_first)
        def _():
            x_via.start()

    p_own = [remote(w_hbm.at[0, pl.ds(h * piece, piece)], w_rows(d, h), psem_s.at[0, h], psem_r.at[0, h], partner) for h in range(pieces)]
    for copy in p_own:
        copy.start()
    p_fwd = [
        [
            remote(w_rows(from_g * 2 + c, h), w_rows(from_g * 2 + c, h), psem_s.at[1 + t, h], psem_r.at[1 + t, h], partner)
            for h in range(pieces)
        ]
        for t, from_g in enumerate(senders)
    ]
    for h in range(pieces):
        for t in range(len(peers)):
            w_out[t][h].wait_recv()
            p_fwd[t][h].start()
    local[0].wait()
    for copies in [p_own] + p_fwd:
        for copy in copies:
            copy.wait_recv()

    relay_f = [remote(fo.at[half[i]], x2.at[half[i]], rsem_s.at[i], rsem_r.at[i], following) for i in range(2)]
    relay_b = [remote(fb.at[half[i]], cots.at[half[2 + i]], rsem_s.at[2 + i], rsem_r.at[2 + i], preceding) for i in range(2)]

    def back_first(i):
        r = half[i]
        backward(kept.at[r], cots.at[r], weights, normed.at[r], hidden.at[r], pre_grad.at[r], fb.at[r], scratch)

    def send_back(i, here):
        pl.when(here & not_first)(relay_b[i].start)

    def ahead_first(i, here):
        @pl.when(here & not_last)
        def _():
            if i:
                m_x.wait_recv()
            r = half[i]
            forward(x1.at[r], fo.at[r], weights, fwd_normed, fwd_hidden)
            relay_f[i].start()

    def back_second(i):
        @pl.when(not_last)
        def _():
            relay_b[i].wait_recv()

        @pl.when(s == sections - 1)
        def _():
            edge_cot[i].wait()

        r = half[2 + i]
        backward(kept.at[r], cots.at[r], weights, normed.at[r], hidden.at[r], pre_grad.at[r], None, None)

    def ahead_second(i):
        forward(x2.at[half[i]], out2.at[half[i]], weights, fwd_normed, fwd_hidden)

    def finish_mirrored():
        ahead_second(1)
        if staged:
            pl.when(outer)(lambda: pl.semaphore_wait(turn, 1))
        pl.when(not_last)(lambda: pl.semaphore_wait(clear, 1))
        m_out.start()

    local[1].wait()
    local[2].wait()
    back_first(0)
    send_back(0, inner if staged else True)
    if staged:

        pl.when(helper)(m_kept2.start)

        @pl.when(helper)
        def _():
            k_via.wait_recv()
            k_pass.start()
    else:
        m_kept2.start()
    m_cot.wait_recv()
    m_kept.wait_recv()
    back_first(1)
    even = lax.rem(s, 2) == 0
    early = even & (s >= sections // 2)
    if staged:
        send_back(0, outer)
        pl.when(outer)(m_kept2.start)
    send_back(1, True)
    if staged:

        @pl.when(inner)
        def _():
            m_x.start()

        @pl.when(inner & (above > 0))
        def _():
            x_via.wait_recv()
            x_pass.start()
    else:
        pl.when(not_first)(m_x.start)
    local[3].wait()
    ahead_first(0, even)
    local[4].wait()
    back_second(0)
    ahead_first(1, early)
    m_kept2.wait_recv()
    back_second(1)

    width = weights.shape[1] // 3
    per = shard // CHUNK

    def term(owner, q, put):
        at = pl.multiple_of(owner * shard + q * CHUNK, CHUNK)
        put(slice(0, 2 * width), lax.dot_general(normed[:, pl.ds(at, CHUNK)], pre_grad[...], TN, preferred_element_type=F32))
        put(slice(2 * width, 3 * width), lax.dot_general(cots[:, pl.ds(at, CHUNK)], hidden[...], TN, preferred_element_type=F32))

    def pair_copy(i):
        return remote(part_send.at[i], part_recv.at[i], gsem_s.at[i], gsem_r.at[i], partner)

    def give(owner_group, i, q):
        def put(columns, value):
            part_send[i, :, columns] = value.astype(BF)

        term(owner_group * 2 + 1 - c, q, put)
        pair_copy(i).start()

    def own_term(owner_group, q, store):
        term(owner_group * 2 + c, q, store)

    def loop(count, body):
        def step(q, carry):
            body(q)
            return carry

        lax.fori_loop(0, count, step, 0)

    def sum_copy(i, to):
        return remote(sum_send.at[i], sum_recv.at[i], ysem_s.at[i], ysem_r.at[i], to)

    for t in range(1, groups):
        to_g = lax.rem(g + t, groups)
        loop(per, lambda q: give(to_g, t * per + q, q))

        def pass_on(q):
            def put(columns, value):
                keep[:, columns] = value

            own_term(to_g, q, put)
            pair_copy(t * per + q).wait_recv()
            i = (t - 1) * per + q
            sum_send[i] = (keep[...] + part_recv[t * per + q].astype(F32)).astype(BF)
            sum_copy(i, peers[t - 1]).start()

        loop(per, pass_on)

    @pl.when(s == 0)
    def _():
        for copy in edge_in:
            copy.wait()
        finish_mirrored()

    own_first = jnp.logical_not(even | middle) if staged else False
    ahead_first(0, own_first)
    ahead_first(1, jnp.logical_not(early))
    ahead_first(0, jnp.logical_not(even | own_first))
    if staged:

        @pl.when(inner)
        def _():
            m_x.wait_send()
            pl.when(above > 0)(x_pass.wait_send)
            pl.semaphore_signal(turn, inc=1, device_id=(above, d), device_id_type=MESH)

    loop(per, lambda q: give(g, q, q))

    def finish(q):
        rows = pl.ds(pl.multiple_of(q * CHUNK, CHUNK), CHUNK)

        def put(columns, value):
            total[rows, columns] = value

        own_term(g, q, put)
        pair_copy(q).wait_recv()
        total[rows] = total[rows] + part_recv[q].astype(F32)

    loop(per, finish)

    @pl.when(not_first)
    def _():
        relay_f[1].wait_recv()
        pl.semaphore_signal(clear, inc=1, device_id=mirror, device_id_type=MESH)
        finish_mirrored()
        relay_f[0].wait_recv()

    ahead_second(0)
    out_own = pltpu.make_async_copy(out2.at[low], out_hbm.at[0, 0], lsem.at[9])
    out_own.start()

    def collect(q):
        rows = pl.ds(pl.multiple_of(q * CHUNK, CHUNK), CHUNK)
        value = total[rows]
        for t in range(1, groups):
            i = (t - 1) * per + q
            sum_copy(i, peers[t - 1]).wait_recv()
            value = value + sum_recv[i].astype(F32)
        total[rows] = value
        pltpu.make_async_copy(total.at[rows], grads_hbm.at[0, rows], lsem.at[10]).start()

    loop(per, collect)
    pltpu.make_async_copy(total, grads_hbm.at[0], lsem.at[10]).wait()

    out_own.wait()
    m_out.wait_recv()
    for copy in (m_cot, m_kept, m_out):
        copy.wait_send()
    if staged:
        for here, copy in ((direct, m_kept2), (middle, k_via), (outer & not_first, x_via), (helper, k_pass)):
            pl.when(here)(copy.wait_send)
    else:
        m_kept2.wait_send()
        pl.when(not_first)(m_x.wait_send)
    for row in w_out + [p_own] + p_fwd:
        for copy in row:
            copy.wait_send()

    @pl.when(not_last)
    def _():
        for copy in relay_f:
            copy.wait_send()

    @pl.when(not_first)
    def _():
        for copy in relay_b:
            copy.wait_send()

    loop(groups * per, lambda i: pair_copy(i).wait_send())
    loop((groups - 1) * per, lambda i: sum_copy(i, peers[0]).wait_send())


def on_device(sections, replicas, x, inc, cot, obj, kept, w):
    span, features = x.shape[2:]
    shard, columns = w.shape[1:]
    width = columns // 3
    groups = replicas // 2
    pairs = groups * (shard // CHUNK)
    sums = max(1, (groups - 1) * (shard // CHUNK))
    dma = pltpu.SemaphoreType.DMA
    v = pltpu.VMEM
    any_space = pl.BlockSpec(memory_space=pl.ANY)
    return pl.pallas_call(
        functools.partial(kernel, sections, replicas),
        out_shape=(
            jax.ShapeDtypeStruct(x.shape, BF),
            jax.ShapeDtypeStruct(w.shape, F32),
        ),
        in_specs=[any_space] * 6,
        out_specs=(any_space, any_space),
        scratch_shapes=[
            v((features, columns), BF),
            v((2 * span, features), BF),
            v((2 * span, features), BF),
            v((4 * span, features), BF),
            v((4 * span, features), BF),
            v((4 * span, features), BF),
            v((4 * span, 2 * width), BF),
            v((4 * span, width), BF),
            v((2 * span, features), BF),
            v((2 * span, features), BF),
            v((2 * span, features), BF),
            v((span, features), BF),
            v((span, width), BF),
            v((span, features), F32),
            v((span, features), BF),
            v((span, features), BF),
            v((pairs, CHUNK, columns), BF),
            v((pairs, CHUNK, columns), BF),
            v((CHUNK, columns), F32),
            v((sums, CHUNK, columns), BF),
            v((sums, CHUNK, columns), BF),
            v((shard, columns), F32),
            dma((11,)),
            dma((groups, 2)),
            dma((groups, 2)),
            dma((groups, 2)),
            dma((groups, 2)),
            dma((5,)),
            dma((5,)),
            dma((4,)),
            dma((4,)),
            dma((pairs,)),
            dma((pairs,)),
            dma((sums,)),
            dma((sums,)),
            dma((4,)),
            dma((2,)),
            pltpu.SemaphoreType.REGULAR,
            pltpu.SemaphoreType.REGULAR,
        ],
        compiler_params=pltpu.CompilerParams(
            collective_id=0, has_side_effects=True, vmem_limit_bytes=60 * 2**20
        ),
    )(x, inc, cot, obj, kept, w)


def solution(mesh):
    in_specs = (
        P(None, "dp", "section", None),
        P(None, "dp", None, None),
        P(None, "dp", "section", None),
        P(None, "dp", None, None),
        P(None, None, "dp", "section", None),
        P("section", "dp", None),
    )
    out_specs = (P(None, "dp", "section", None), P("section", "dp", None))
    body = functools.partial(on_device, mesh.shape["section"], mesh.shape["dp"])
    return jax.shard_map(body, mesh=mesh, in_specs=in_specs, out_specs=out_specs, check_vma=False)
```

```python
import functools

import jax
import jax.numpy as jnp
from jax import lax
from jax.experimental import pallas as pl
from jax.experimental.pallas import tpu as pltpu
from jax.sharding import PartitionSpec as P

MESH = pl.DeviceIdType.MESH
BF = jnp.bfloat16
F32 = jnp.float32
TILE = 256
CHUNK = 128
NT = (((1,), (1,)), ((), ()))
TN = (((0,), (0,)), ((), ()))


def normalize_into(src, dst):
    values = src[...].astype(F32)
    inverse = lax.rsqrt(jnp.mean(values * values, axis=-1, keepdims=True) + 1e-06)
    dst[...] = (values * inverse).astype(BF)
    return inverse


def tiles(count, body):
    def step(j, carry):
        body(pl.multiple_of(j * TILE, TILE))
        return carry

    lax.fori_loop(0, count // TILE, step, 0)


def forward(rows, out, weights, normed, hidden):
    width = weights.shape[1] // 3
    normalize_into(rows, normed)

    def hidden_tile(at):
        gate = jnp.dot(normed[...], weights[:, pl.ds(at, TILE)], preferred_element_type=F32)
        up = jnp.dot(normed[...], weights[:, pl.ds(width + at, TILE)], preferred_element_type=F32)
        hidden[:, pl.ds(at, TILE)] = (gate * jax.nn.sigmoid(gate) * up).astype(BF)

    tiles(width, hidden_tile)

    def out_tile(at):
        branch = lax.dot_general(
            hidden[...], weights[pl.ds(at, TILE), 2 * width :], NT, preferred_element_type=F32
        )
        out[:, pl.ds(at, TILE)] = (rows[:, pl.ds(at, TILE)].astype(F32) + branch).astype(BF)

    tiles(weights.shape[0], out_tile)


def backward(rows, cotangent, weights, normed, hidden, pre_grad, back, scratch):
    width = weights.shape[1] // 3
    inverse = normalize_into(rows, normed)

    def hidden_tile(at):
        gate = jnp.dot(normed[...], weights[:, pl.ds(at, TILE)], preferred_element_type=F32)
        up = jnp.dot(normed[...], weights[:, pl.ds(width + at, TILE)], preferred_element_type=F32)
        grad = jnp.dot(
            cotangent[...], weights[:, pl.ds(2 * width + at, TILE)], preferred_element_type=F32
        )
        sig = jax.nn.sigmoid(gate)
        silu = gate * sig
        hidden[:, pl.ds(at, TILE)] = (silu * up).astype(BF)
        pre_grad[:, pl.ds(at, TILE)] = (grad * up * sig * (1.0 + gate * (1.0 - sig))).astype(BF)
        pre_grad[:, pl.ds(width + at, TILE)] = (grad * silu).astype(BF)

    tiles(width, hidden_tile)
    if back is None:
        return

    def grad_tile(at):
        scratch[:, pl.ds(at, TILE)] = lax.dot_general(
            pre_grad[...], weights[pl.ds(at, TILE), : 2 * width], NT, preferred_element_type=F32
        )

    tiles(weights.shape[0], grad_tile)
    values = rows[...].astype(F32)
    grad = scratch[...]
    inner = jnp.mean(grad * values, axis=-1, keepdims=True)
    back[...] = (
        cotangent[...].astype(F32)
        + inverse * grad
        - values * (inverse * inverse * inverse * inner)
    ).astype(BF)


def kernel(
    sections, replicas,
    x_hbm, inc_hbm, cot_hbm, obj_hbm, kept_hbm, w_hbm,
    out_hbm, grads_hbm,
    weights, x1, x2, kept, cots, normed, pre_grad, hidden, fo, fb, out2,
    fwd_normed, fwd_hidden, scratch, via_kept, via_x,
    part_send, part_recv, keep, sum_send, sum_recv, total,
    lsem, wsem_s, wsem_r, psem_s, psem_r, msem_s, msem_r, rsem_s, rsem_r, gsem_s, gsem_r, ysem_s, ysem_r, vsem_s, vsem_r, turn, clear,
):
    s = lax.axis_index("section")
    d = lax.axis_index("dp")
    span = x1.shape[0] // 2
    shard = w_hbm.shape[1]
    groups = replicas // 2
    g, c = d // 2, lax.rem(d, 2)
    partner = (s, g * 2 + 1 - c)
    mirror = (sections - 1 - s, d)
    not_first = s > 0
    not_last = s < sections - 1
    peers = [(s, lax.rem(g + t, groups) * 2 + c) for t in range(1, groups)]
    senders = [lax.rem(g - t + groups, groups) for t in range(1, groups)]

    def remote(src, dst, ss, rs, to):
        return pltpu.make_async_remote_copy(
            src_ref=src, dst_ref=dst, send_sem=ss, recv_sem=rs, device_id=to, device_id_type=MESH
        )

    low, high = pl.ds(0, span), pl.ds(span, span)
    half = [pl.ds(i * span, span) for i in range(4)]

    local = [
        (w_hbm.at[0], weights.at[pl.ds(pl.multiple_of(d * shard, shard), shard)]),
        (cot_hbm.at[0, 0], cots.at[half[0]]),
        (kept_hbm.at[0, 0, 0], kept.at[half[0]]),
        (x_hbm.at[0, 0], x1.at[low]),
        (kept_hbm.at[0, 1, 0], kept.at[half[2]]),
    ]
    local = [pltpu.make_async_copy(a, b, lsem.at[i]) for i, (a, b) in enumerate(local)]
    for copy in local:
        copy.start()
    edge_in = [pltpu.make_async_copy(inc_hbm.at[i, 0], x2.at[half[i]], lsem.at[5 + i]) for i in range(2)]
    edge_cot = [
        pltpu.make_async_copy(obj_hbm.at[i, 0], cots.at[half[2 + i]], lsem.at[7 + i]) for i in range(2)
    ]

    @pl.when(s == 0)
    def _():
        for copy in edge_in:
            copy.start()

    @pl.when(s == sections - 1)
    def _():
        for copy in edge_cot:
            copy.start()

    following = (lax.rem(s + 1, sections), d)
    preceding = (lax.rem(s + sections - 1, sections), d)
    staged = sections == 8
    greeted = [mirror, partner, following, preceding] + peers
    if staged:
        above = s + 2 - 4 * lax.rem(s // 2, 2)
        beside = s + 1 - 2 * lax.rem(s, 2)
        outer = (s < 2) | (s >= sections - 2)
        inner = (s >= 2) & (s < sections - 2)
        middle = (s == sections // 2 - 1) | (s == sections // 2)
        helper = (s == sections // 2 - 2) | (s == sections // 2 + 1)
        direct = (s < sections // 2 - 1) | (s > sections // 2)
        greeted += [(above, d), (sections - 1 - above, d), (sections - 1 - beside, d)]
    barrier = pltpu.get_barrier_semaphore()
    for to in greeted:
        pl.semaphore_signal(barrier, inc=1, device_id=to, device_id_type=MESH)
    pl.semaphore_wait(barrier, len(greeted))

    pieces = 2
    piece = shard // pieces

    def w_rows(owner, h):
        return weights.at[pl.ds(pl.multiple_of(owner * shard + h * piece, piece), piece)]

    w_out = [
        [remote(w_hbm.at[0, pl.ds(h * piece, piece)], w_rows(d, h), wsem_s.at[t, h], wsem_r.at[t, h], to) for h in range(pieces)]
        for t, to in enumerate(peers)
    ]
    for h in range(pieces):
        for row in w_out:
            row[h].start()

    def mirrored(src, dst, i):
        return remote(src, dst, msem_s.at[i], msem_r.at[i], mirror)

    m_cot = mirrored(cot_hbm.at[1, 0], cots.at[half[1]], 0)
    m_kept = mirrored(kept_hbm.at[1, 0, 0], kept.at[half[1]], 1)
    m_x = mirrored(x_hbm.at[1, 0], x1.at[high], 2)
    m_kept2 = mirrored(kept_hbm.at[1, 1, 0], kept.at[half[3]], 3)
    m_out = mirrored(out2.at[high], out_hbm.at[1, 0], 4)
    m_cot.start()
    m_kept.start()
    if staged:
        k_via = remote(kept_hbm.at[1, 1, 0], via_kept, vsem_s.at[0], vsem_r.at[0], (beside, d))
        x_via = remote(x_hbm.at[1, 0], via_x, vsem_s.at[1], vsem_r.at[1], (above, d))
        k_pass = remote(via_kept, kept.at[half[3]], vsem_s.at[2], msem_r.at[3], (sections - 1 - beside, d))
        x_pass = remote(via_x, x1.at[high], vsem_s.at[3], msem_r.at[2], (sections - 1 - above, d))

        @pl.when(middle)
        def _():
            k_via.start()

        @pl.when(outer & not_first)
        def _():
            x_via.start()

    p_own = [remote(w_hbm.at[0, pl.ds(h * piece, piece)], w_rows(d, h), psem_s.at[0, h], psem_r.at[0, h], partner) for h in range(pieces)]
    for copy in p_own:
        copy.start()
    p_fwd = [
        [
            remote(w_rows(from_g * 2 + c, h), w_rows(from_g * 2 + c, h), psem_s.at[1 + t, h], psem_r.at[1 + t, h], partner)
            for h in range(pieces)
        ]
        for t, from_g in enumerate(senders)
    ]
    for h in range(pieces):
        for t in range(len(peers)):
            w_out[t][h].wait_recv()
            p_fwd[t][h].start()
    local[0].wait()
    for copies in [p_own] + p_fwd:
        for copy in copies:
            copy.wait_recv()

    relay_f = [remote(fo.at[half[i]], x2.at[half[i]], rsem_s.at[i], rsem_r.at[i], following) for i in range(2)]
    relay_b = [remote(fb.at[half[i]], cots.at[half[2 + i]], rsem_s.at[2 + i], rsem_r.at[2 + i], preceding) for i in range(2)]

    def back_first(i):
        r = half[i]
        backward(kept.at[r], cots.at[r], weights, normed.at[r], hidden.at[r], pre_grad.at[r], fb.at[r], scratch)

    def send_back(i, here):
        pl.when(here & not_first)(relay_b[i].start)

    def ahead_first(i, here):
        @pl.when(here & not_last)
        def _():
            if i:
                m_x.wait_recv()
            r = half[i]
            forward(x1.at[r], fo.at[r], weights, fwd_normed, fwd_hidden)
            relay_f[i].start()

    def back_second(i):
        @pl.when(not_last)
        def _():
            relay_b[i].wait_recv()

        @pl.when(s == sections - 1)
        def _():
            edge_cot[i].wait()

        r = half[2 + i]
        backward(kept.at[r], cots.at[r], weights, normed.at[r], hidden.at[r], pre_grad.at[r], None, None)

    def ahead_second(i):
        forward(x2.at[half[i]], out2.at[half[i]], weights, fwd_normed, fwd_hidden)

    def finish_mirrored():
        ahead_second(1)
        if staged:
            pl.when(outer)(lambda: pl.semaphore_wait(turn, 1))
        pl.when(not_last)(lambda: pl.semaphore_wait(clear, 1))
        m_out.start()

    local[1].wait()
    local[2].wait()
    back_first(0)
    send_back(0, inner if staged else True)
    if staged:

        pl.when(helper)(m_kept2.start)

        @pl.when(helper)
        def _():
            k_via.wait_recv()
            k_pass.start()
    else:
        m_kept2.start()
    m_cot.wait_recv()
    m_kept.wait_recv()
    back_first(1)
    even = lax.rem(s, 2) == 0
    early = even & (s >= sections // 2)
    crossing = jnp.logical_not(even) & middle if staged else False
    if staged:
        send_back(0, outer)
        pl.when(outer)(m_kept2.start)
    send_back(1, True)
    if staged:

        @pl.when(inner)
        def _():
            m_x.start()

        @pl.when(inner & (above > 0))
        def _():
            x_via.wait_recv()
            x_pass.start()
    else:
        pl.when(not_first)(m_x.start)
    local[3].wait()
    ahead_first(0, even)
    local[4].wait()
    back_second(0)
    if staged:
        ahead_first(0, crossing)
    ahead_first(1, early)
    m_kept2.wait_recv()
    back_second(1)

    width = weights.shape[1] // 3
    per = shard // CHUNK

    def term(owner, q, put):
        at = pl.multiple_of(owner * shard + q * CHUNK, CHUNK)
        put(slice(0, 2 * width), lax.dot_general(normed[:, pl.ds(at, CHUNK)], pre_grad[...], TN, preferred_element_type=F32))
        put(slice(2 * width, 3 * width), lax.dot_general(cots[:, pl.ds(at, CHUNK)], hidden[...], TN, preferred_element_type=F32))

    def pair_copy(i):
        return remote(part_send.at[i], part_recv.at[i], gsem_s.at[i], gsem_r.at[i], partner)

    def give(owner_group, i, q):
        def put(columns, value):
            part_send[i, :, columns] = value.astype(BF)

        term(owner_group * 2 + 1 - c, q, put)
        pair_copy(i).start()

    def own_term(owner_group, q, store):
        term(owner_group * 2 + c, q, store)

    def loop(count, body):
        def step(q, carry):
            body(q)
            return carry

        lax.fori_loop(0, count, step, 0)

    def sum_copy(i, to):
        return remote(sum_send.at[i], sum_recv.at[i], ysem_s.at[i], ysem_r.at[i], to)

    for t in range(1, groups):
        to_g = lax.rem(g + t, groups)
        loop(per, lambda q: give(to_g, t * per + q, q))

        def pass_on(q):
            def put(columns, value):
                keep[:, columns] = value

            own_term(to_g, q, put)
            pair_copy(t * per + q).wait_recv()
            i = (t - 1) * per + q
            sum_send[i] = (keep[...] + part_recv[t * per + q].astype(F32)).astype(BF)
            sum_copy(i, peers[t - 1]).start()

        loop(per, pass_on)

    @pl.when(s == 0)
    def _():
        for copy in edge_in:
            copy.wait()
        finish_mirrored()

    ahead_first(0, jnp.logical_not(even | crossing))
    ahead_first(1, jnp.logical_not(early))
    if staged:

        @pl.when(inner)
        def _():
            m_x.wait_send()
            pl.when(above > 0)(x_pass.wait_send)
            pl.semaphore_signal(turn, inc=1, device_id=(above, d), device_id_type=MESH)

    loop(per, lambda q: give(g, q, q))

    def finish(q):
        rows = pl.ds(pl.multiple_of(q * CHUNK, CHUNK), CHUNK)

        def put(columns, value):
            total[rows, columns] = value

        own_term(g, q, put)
        pair_copy(q).wait_recv()
        total[rows] = total[rows] + part_recv[q].astype(F32)

    loop(per, finish)

    @pl.when(not_first)
    def _():
        relay_f[1].wait_recv()
        pl.semaphore_signal(clear, inc=1, device_id=mirror, device_id_type=MESH)
        finish_mirrored()
        relay_f[0].wait_recv()

    ahead_second(0)
    out_own = pltpu.make_async_copy(out2.at[low], out_hbm.at[0, 0], lsem.at[9])
    out_own.start()

    def collect(q):
        rows = pl.ds(pl.multiple_of(q * CHUNK, CHUNK), CHUNK)
        value = total[rows]
        for t in range(1, groups):
            i = (t - 1) * per + q
            sum_copy(i, peers[t - 1]).wait_recv()
            value = value + sum_recv[i].astype(F32)
        total[rows] = value
        pltpu.make_async_copy(total.at[rows], grads_hbm.at[0, rows], lsem.at[10]).start()

    loop(per, collect)
    pltpu.make_async_copy(total, grads_hbm.at[0], lsem.at[10]).wait()

    out_own.wait()
    m_out.wait_recv()
    for copy in (m_cot, m_kept, m_out):
        copy.wait_send()
    if staged:
        for here, copy in ((direct, m_kept2), (middle, k_via), (outer & not_first, x_via), (helper, k_pass)):
            pl.when(here)(copy.wait_send)
    else:
        m_kept2.wait_send()
        pl.when(not_first)(m_x.wait_send)
    for row in w_out + [p_own] + p_fwd:
        for copy in row:
            copy.wait_send()

    @pl.when(not_last)
    def _():
        for copy in relay_f:
            copy.wait_send()

    @pl.when(not_first)
    def _():
        for copy in relay_b:
            copy.wait_send()

    loop(groups * per, lambda i: pair_copy(i).wait_send())
    loop((groups - 1) * per, lambda i: sum_copy(i, peers[0]).wait_send())


def on_device(sections, replicas, x, inc, cot, obj, kept, w):
    span, features = x.shape[2:]
    shard, columns = w.shape[1:]
    width = columns // 3
    groups = replicas // 2
    pairs = groups * (shard // CHUNK)
    sums = max(1, (groups - 1) * (shard // CHUNK))
    dma = pltpu.SemaphoreType.DMA
    v = pltpu.VMEM
    any_space = pl.BlockSpec(memory_space=pl.ANY)
    results = pl.pallas_call(
        functools.partial(kernel, sections, replicas),
        out_shape=(
            jax.ShapeDtypeStruct(x.shape, BF),
            jax.ShapeDtypeStruct(w.shape, F32),
        ),
        in_specs=[any_space] * 6,
        out_specs=(any_space, any_space),
        scratch_shapes=[
            v((features, columns), BF),
            v((2 * span, features), BF),
            v((2 * span, features), BF),
            v((4 * span, features), BF),
            v((4 * span, features), BF),
            v((4 * span, features), BF),
            v((4 * span, 2 * width), BF),
            v((4 * span, width), BF),
            v((2 * span, features), BF),
            v((2 * span, features), BF),
            v((2 * span, features), BF),
            v((span, features), BF),
            v((span, width), BF),
            v((span, features), F32),
            v((span, features), BF),
            v((span, features), BF),
            v((pairs, CHUNK, columns), BF),
            v((pairs, CHUNK, columns), BF),
            v((CHUNK, columns), F32),
            v((sums, CHUNK, columns), BF),
            v((sums, CHUNK, columns), BF),
            v((shard, columns), F32),
            dma((11,)),
            dma((groups, 2)),
            dma((groups, 2)),
            dma((groups, 2)),
            dma((groups, 2)),
            dma((5,)),
            dma((5,)),
            dma((4,)),
            dma((4,)),
            dma((pairs,)),
            dma((pairs,)),
            dma((sums,)),
            dma((sums,)),
            dma((4,)),
            dma((2,)),
            pltpu.SemaphoreType.REGULAR,
            pltpu.SemaphoreType.REGULAR,
        ],
        compiler_params=pltpu.CompilerParams(
            collective_id=0, has_side_effects=True, vmem_limit_bytes=60 * 2**20
        ),
    )(x, inc, cot, obj, kept, w)
    return hand_out(*results)


def hand_out(out, grads):
    steps = 4
    rows = grads.shape[1] // steps
    count = steps + out.shape[0]

    def body(out_ref, grads_ref, out_to, grads_to, out_mid, grads_mid, sem_in, sem_out):
        parts = [(grads_ref, grads_mid, grads_to, (0, pl.ds(i * rows, rows))) for i in range(steps)]
        parts += [(out_ref, out_mid, out_to, (i,)) for i in range(out.shape[0])]
        taken = [pltpu.make_async_copy(a.at[at], b.at[at], sem_in.at[i]) for i, (a, b, _, at) in enumerate(parts)]
        given = [pltpu.make_async_copy(b.at[at], c.at[at], sem_out.at[i]) for i, (_, b, c, at) in enumerate(parts)]
        for copy in taken:
            copy.start()
        for one, two in zip(taken, given):
            one.wait()
            two.start()
        for copy in given:
            copy.wait()

    any_space = pl.BlockSpec(memory_space=pl.ANY)
    return pl.pallas_call(
        body,
        out_shape=(
            jax.ShapeDtypeStruct(out.shape, out.dtype),
            jax.ShapeDtypeStruct(grads.shape, grads.dtype),
        ),
        in_specs=[any_space] * 2,
        out_specs=(any_space, any_space),
        scratch_shapes=[
            pltpu.VMEM(out.shape, out.dtype),
            pltpu.VMEM(grads.shape, grads.dtype),
            pltpu.SemaphoreType.DMA((count,)),
            pltpu.SemaphoreType.DMA((count,)),
        ],
    )(out, grads)


def solution(mesh):
    in_specs = (
        P(None, "dp", "section", None),
        P(None, "dp", None, None),
        P(None, "dp", "section", None),
        P(None, "dp", None, None),
        P(None, None, "dp", "section", None),
        P("section", "dp", None),
    )
    out_specs = (P(None, "dp", "section", None), P("section", "dp", None))
    body = functools.partial(on_device, mesh.shape["section"], mesh.shape["dp"])
    return jax.shard_map(body, mesh=mesh, in_specs=in_specs, out_specs=out_specs, check_vma=False)
```

```python
import functools

import jax
import jax.numpy as jnp
from jax import lax
from jax.experimental import pallas as pl
from jax.experimental.pallas import tpu as pltpu
from jax.sharding import PartitionSpec as P

MESH = pl.DeviceIdType.MESH
BF = jnp.bfloat16
F32 = jnp.float32
TILE = 256
CHUNK = 128
NT = (((1,), (1,)), ((), ()))
TN = (((0,), (0,)), ((), ()))


def normalize_into(src, dst):
    values = src[...].astype(F32)
    inverse = lax.rsqrt(jnp.mean(values * values, axis=-1, keepdims=True) + 1e-06)
    dst[...] = (values * inverse).astype(BF)
    return inverse


def tiles(count, body):
    def step(j, carry):
        body(pl.multiple_of(j * TILE, TILE))
        return carry

    lax.fori_loop(0, count // TILE, step, 0)


def forward(rows, out, weights, normed, hidden):
    width = weights.shape[1] // 3
    normalize_into(rows, normed)

    def hidden_tile(at):
        gate = jnp.dot(normed[...], weights[:, pl.ds(at, TILE)], preferred_element_type=F32)
        up = jnp.dot(normed[...], weights[:, pl.ds(width + at, TILE)], preferred_element_type=F32)
        hidden[:, pl.ds(at, TILE)] = (gate * jax.nn.sigmoid(gate) * up).astype(BF)

    tiles(width, hidden_tile)

    def out_tile(at):
        branch = lax.dot_general(
            hidden[...], weights[pl.ds(at, TILE), 2 * width :], NT, preferred_element_type=F32
        )
        out[:, pl.ds(at, TILE)] = (rows[:, pl.ds(at, TILE)].astype(F32) + branch).astype(BF)

    tiles(weights.shape[0], out_tile)


def backward(rows, cotangent, weights, normed, hidden, pre_grad, back, scratch):
    width = weights.shape[1] // 3
    inverse = normalize_into(rows, normed)

    def hidden_tile(at):
        gate = jnp.dot(normed[...], weights[:, pl.ds(at, TILE)], preferred_element_type=F32)
        up = jnp.dot(normed[...], weights[:, pl.ds(width + at, TILE)], preferred_element_type=F32)
        grad = jnp.dot(
            cotangent[...], weights[:, pl.ds(2 * width + at, TILE)], preferred_element_type=F32
        )
        sig = jax.nn.sigmoid(gate)
        silu = gate * sig
        hidden[:, pl.ds(at, TILE)] = (silu * up).astype(BF)
        pre_grad[:, pl.ds(at, TILE)] = (grad * up * sig * (1.0 + gate * (1.0 - sig))).astype(BF)
        pre_grad[:, pl.ds(width + at, TILE)] = (grad * silu).astype(BF)

    tiles(width, hidden_tile)
    if back is None:
        return

    def grad_tile(at):
        scratch[:, pl.ds(at, TILE)] = lax.dot_general(
            pre_grad[...], weights[pl.ds(at, TILE), : 2 * width], NT, preferred_element_type=F32
        )

    tiles(weights.shape[0], grad_tile)
    values = rows[...].astype(F32)
    grad = scratch[...]
    inner = jnp.mean(grad * values, axis=-1, keepdims=True)
    back[...] = (
        cotangent[...].astype(F32)
        + inverse * grad
        - values * (inverse * inverse * inverse * inner)
    ).astype(BF)


def kernel(
    sections, replicas,
    x_hbm, inc_hbm, cot_hbm, obj_hbm, kept_hbm, w_hbm,
    out_hbm, grads_hbm,
    weights, x1, x2, kept, cots, normed, pre_grad, hidden, fo, fb, out2,
    fwd_normed, fwd_hidden, scratch, via_kept, via_x,
    part_send, part_recv, keep, sum_send, sum_recv, total,
    lsem, wsem_s, wsem_r, psem_s, psem_r, msem_s, msem_r, rsem_s, rsem_r, gsem_s, gsem_r, ysem_s, ysem_r, vsem_s, vsem_r, turn, clear,
):
    s = lax.axis_index("section")
    d = lax.axis_index("dp")
    span = x1.shape[0] // 2
    shard = w_hbm.shape[1]
    groups = replicas // 2
    g, c = d // 2, lax.rem(d, 2)
    partner = (s, g * 2 + 1 - c)
    mirror = (sections - 1 - s, d)
    not_first = s > 0
    not_last = s < sections - 1
    peers = [(s, lax.rem(g + t, groups) * 2 + c) for t in range(1, groups)]
    senders = [lax.rem(g - t + groups, groups) for t in range(1, groups)]

    def remote(src, dst, ss, rs, to):
        return pltpu.make_async_remote_copy(
            src_ref=src, dst_ref=dst, send_sem=ss, recv_sem=rs, device_id=to, device_id_type=MESH
        )

    low, high = pl.ds(0, span), pl.ds(span, span)
    half = [pl.ds(i * span, span) for i in range(4)]

    local = [
        (w_hbm.at[0], weights.at[pl.ds(pl.multiple_of(d * shard, shard), shard)]),
        (cot_hbm.at[0, 0], cots.at[half[0]]),
        (kept_hbm.at[0, 0, 0], kept.at[half[0]]),
        (x_hbm.at[0, 0], x1.at[low]),
        (kept_hbm.at[0, 1, 0], kept.at[half[2]]),
    ]
    local = [pltpu.make_async_copy(a, b, lsem.at[i]) for i, (a, b) in enumerate(local)]
    for copy in local:
        copy.start()
    edge_in = [pltpu.make_async_copy(inc_hbm.at[i, 0], x2.at[half[i]], lsem.at[5 + i]) for i in range(2)]
    edge_cot = [
        pltpu.make_async_copy(obj_hbm.at[i, 0], cots.at[half[2 + i]], lsem.at[7 + i]) for i in range(2)
    ]

    @pl.when(s == 0)
    def _():
        for copy in edge_in:
            copy.start()

    @pl.when(s == sections - 1)
    def _():
        for copy in edge_cot:
            copy.start()

    following = (lax.rem(s + 1, sections), d)
    preceding = (lax.rem(s + sections - 1, sections), d)
    staged = sections == 8
    greeted = [mirror, partner, following, preceding] + peers
    if staged:
        above = s + 2 - 4 * lax.rem(s // 2, 2)
        beside = s + 1 - 2 * lax.rem(s, 2)
        outer = (s < 2) | (s >= sections - 2)
        inner = (s >= 2) & (s < sections - 2)
        middle = (s == sections // 2 - 1) | (s == sections // 2)
        helper = (s == sections // 2 - 2) | (s == sections // 2 + 1)
        direct = (s < sections // 2 - 1) | (s > sections // 2)
        greeted += [(above, d), (sections - 1 - above, d), (sections - 1 - beside, d)]
    barrier = pltpu.get_barrier_semaphore()
    for to in greeted:
        pl.semaphore_signal(barrier, inc=1, device_id=to, device_id_type=MESH)
    pl.semaphore_wait(barrier, len(greeted))

    pieces = 2
    piece = shard // pieces

    def w_rows(owner, h):
        return weights.at[pl.ds(pl.multiple_of(owner * shard + h * piece, piece), piece)]

    w_out = [
        [remote(w_hbm.at[0, pl.ds(h * piece, piece)], w_rows(d, h), wsem_s.at[t, h], wsem_r.at[t, h], to) for h in range(pieces)]
        for t, to in enumerate(peers)
    ]
    for h in range(pieces):
        for row in w_out:
            row[h].start()

    def mirrored(src, dst, i):
        return remote(src, dst, msem_s.at[i], msem_r.at[i], mirror)

    m_cot = mirrored(cot_hbm.at[1, 0], cots.at[half[1]], 0)
    m_kept = mirrored(kept_hbm.at[1, 0, 0], kept.at[half[1]], 1)
    m_x = mirrored(x_hbm.at[1, 0], x1.at[high], 2)
    m_kept2 = mirrored(kept_hbm.at[1, 1, 0], kept.at[half[3]], 3)
    m_out = mirrored(out2.at[high], out_hbm.at[1, 0], 4)
    m_cot.start()
    m_kept.start()
    if staged:
        k_via = remote(kept_hbm.at[1, 1, 0], via_kept, vsem_s.at[0], vsem_r.at[0], (beside, d))
        x_via = remote(x_hbm.at[1, 0], via_x, vsem_s.at[1], vsem_r.at[1], (above, d))
        k_pass = remote(via_kept, kept.at[half[3]], vsem_s.at[2], msem_r.at[3], (sections - 1 - beside, d))
        x_pass = remote(via_x, x1.at[high], vsem_s.at[3], msem_r.at[2], (sections - 1 - above, d))

        @pl.when(middle)
        def _():
            k_via.start()

        @pl.when(outer & not_first)
        def _():
            x_via.start()

    p_own = [remote(w_hbm.at[0, pl.ds(h * piece, piece)], w_rows(d, h), psem_s.at[0, h], psem_r.at[0, h], partner) for h in range(pieces)]
    for copy in p_own:
        copy.start()
    p_fwd = [
        [
            remote(w_rows(from_g * 2 + c, h), w_rows(from_g * 2 + c, h), psem_s.at[1 + t, h], psem_r.at[1 + t, h], partner)
            for h in range(pieces)
        ]
        for t, from_g in enumerate(senders)
    ]
    for h in range(pieces):
        for t in range(len(peers)):
            w_out[t][h].wait_recv()
            p_fwd[t][h].start()
    local[0].wait()
    for copies in [p_own] + p_fwd:
        for copy in copies:
            copy.wait_recv()

    relay_f = [remote(fo.at[half[i]], x2.at[half[i]], rsem_s.at[i], rsem_r.at[i], following) for i in range(2)]
    relay_b = [remote(fb.at[half[i]], cots.at[half[2 + i]], rsem_s.at[2 + i], rsem_r.at[2 + i], preceding) for i in range(2)]

    def back_first(i):
        r = half[i]
        backward(kept.at[r], cots.at[r], weights, normed.at[r], hidden.at[r], pre_grad.at[r], fb.at[r], scratch)

    def send_back(i, here):
        pl.when(here & not_first)(relay_b[i].start)

    def ahead_first(i, here):
        @pl.when(here & not_last)
        def _():
            if i:
                m_x.wait_recv()
            r = half[i]
            forward(x1.at[r], fo.at[r], weights, fwd_normed, fwd_hidden)
            relay_f[i].start()

    def back_second(i):
        @pl.when(not_last)
        def _():
            relay_b[i].wait_recv()

        @pl.when(s == sections - 1)
        def _():
            edge_cot[i].wait()

        r = half[2 + i]
        backward(kept.at[r], cots.at[r], weights, normed.at[r], hidden.at[r], pre_grad.at[r], None, None)

    def ahead_second(i):
        forward(x2.at[half[i]], out2.at[half[i]], weights, fwd_normed, fwd_hidden)

    def finish_mirrored():
        ahead_second(1)
        if staged:
            pl.when(outer)(lambda: pl.semaphore_wait(turn, 1))
        pl.when(not_last)(lambda: pl.semaphore_wait(clear, 1))
        m_out.start()

    local[1].wait()
    local[2].wait()
    back_first(0)
    send_back(0, inner if staged else True)
    if staged:

        pl.when(helper)(m_kept2.start)

        @pl.when(helper)
        def _():
            k_via.wait_recv()
            k_pass.start()
    else:
        m_kept2.start()
    m_cot.wait_recv()
    m_kept.wait_recv()
    back_first(1)
    even = lax.rem(s, 2) == 0
    early = even & (s >= sections // 2)
    crossing = jnp.logical_not(even) & middle if staged else False
    if staged:
        send_back(0, outer)
        pl.when(outer)(m_kept2.start)
    send_back(1, True)
    if staged:

        @pl.when(inner)
        def _():
            m_x.start()

        @pl.when(inner & (above > 0))
        def _():
            x_via.wait_recv()
            x_pass.start()
    else:
        pl.when(not_first)(m_x.start)
    local[3].wait()
    ahead_first(0, even)
    local[4].wait()
    back_second(0)
    if staged:
        ahead_first(0, crossing)
    ahead_first(1, early)
    m_kept2.wait_recv()
    back_second(1)

    width = weights.shape[1] // 3
    per = shard // CHUNK

    def term(owner, q, put):
        at = pl.multiple_of(owner * shard + q * CHUNK, CHUNK)
        put(slice(0, 2 * width), lax.dot_general(normed[:, pl.ds(at, CHUNK)], pre_grad[...], TN, preferred_element_type=F32))
        put(slice(2 * width, 3 * width), lax.dot_general(cots[:, pl.ds(at, CHUNK)], hidden[...], TN, preferred_element_type=F32))

    def pair_copy(i):
        return remote(part_send.at[i], part_recv.at[i], gsem_s.at[i], gsem_r.at[i], partner)

    def give(owner_group, i, q):
        def put(columns, value):
            part_send[i, :, columns] = value.astype(BF)

        term(owner_group * 2 + 1 - c, q, put)
        pair_copy(i).start()

    def own_term(owner_group, q, store):
        term(owner_group * 2 + c, q, store)

    def loop(count, body):
        def step(q, carry):
            body(q)
            return carry

        lax.fori_loop(0, count, step, 0)

    def sum_copy(i, to):
        return remote(sum_send.at[i], sum_recv.at[i], ysem_s.at[i], ysem_r.at[i], to)

    for t in range(1, groups):
        to_g = lax.rem(g + t, groups)
        loop(per, lambda q: give(to_g, t * per + q, q))

        def pass_on(q):
            def put(columns, value):
                keep[:, columns] = value

            own_term(to_g, q, put)
            pair_copy(t * per + q).wait_recv()
            i = (t - 1) * per + q
            sum_send[i] = (keep[...] + part_recv[t * per + q].astype(F32)).astype(BF)
            sum_copy(i, peers[t - 1]).start()

        loop(per, pass_on)

    @pl.when(s == 0)
    def _():
        for copy in edge_in:
            copy.wait()
        finish_mirrored()

    ahead_first(0, jnp.logical_not(even | crossing))
    ahead_first(1, jnp.logical_not(early))
    if staged:

        @pl.when(inner)
        def _():
            m_x.wait_send()
            pl.when(above > 0)(x_pass.wait_send)
            pl.semaphore_signal(turn, inc=1, device_id=(above, d), device_id_type=MESH)

    loop(per, lambda q: give(g, q, q))

    def finish(q):
        rows = pl.ds(pl.multiple_of(q * CHUNK, CHUNK), CHUNK)

        def put(columns, value):
            total[rows, columns] = value

        own_term(g, q, put)
        pair_copy(q).wait_recv()
        total[rows] = total[rows] + part_recv[q].astype(F32)

    loop(per, finish)

    @pl.when(not_first)
    def _():
        relay_f[1].wait_recv()
        pl.semaphore_signal(clear, inc=1, device_id=mirror, device_id_type=MESH)
        finish_mirrored()
        relay_f[0].wait_recv()

    ahead_second(0)
    out_own = pltpu.make_async_copy(out2.at[low], out_hbm.at[0, 0], lsem.at[9])
    out_own.start()

    def collect(q):
        rows = pl.ds(pl.multiple_of(q * CHUNK, CHUNK), CHUNK)
        value = total[rows]
        for t in range(1, groups):
            i = (t - 1) * per + q
            sum_copy(i, peers[t - 1]).wait_recv()
            value = value + sum_recv[i].astype(F32)
        total[rows] = value
        pltpu.make_async_copy(total.at[rows], grads_hbm.at[0, rows], lsem.at[10]).start()

    loop(per, collect)
    pltpu.make_async_copy(total, grads_hbm.at[0], lsem.at[10]).wait()

    out_own.wait()
    m_out.wait_recv()
    for copy in (m_cot, m_kept, m_out):
        copy.wait_send()
    if staged:
        for here, copy in ((direct, m_kept2), (middle, k_via), (outer & not_first, x_via), (helper, k_pass)):
            pl.when(here)(copy.wait_send)
    else:
        m_kept2.wait_send()
        pl.when(not_first)(m_x.wait_send)
    for row in w_out + [p_own] + p_fwd:
        for copy in row:
            copy.wait_send()

    @pl.when(not_last)
    def _():
        for copy in relay_f:
            copy.wait_send()

    @pl.when(not_first)
    def _():
        for copy in relay_b:
            copy.wait_send()

    loop(groups * per, lambda i: pair_copy(i).wait_send())
    loop((groups - 1) * per, lambda i: sum_copy(i, peers[0]).wait_send())


def on_device(sections, replicas, x, inc, cot, obj, kept, w):
    span, features = x.shape[2:]
    shard, columns = w.shape[1:]
    width = columns // 3
    groups = replicas // 2
    pairs = groups * (shard // CHUNK)
    sums = max(1, (groups - 1) * (shard // CHUNK))
    dma = pltpu.SemaphoreType.DMA
    v = pltpu.VMEM
    any_space = pl.BlockSpec(memory_space=pl.ANY)
    results = pl.pallas_call(
        functools.partial(kernel, sections, replicas),
        out_shape=(
            jax.ShapeDtypeStruct(x.shape, BF),
            jax.ShapeDtypeStruct(w.shape, F32),
        ),
        in_specs=[any_space] * 6,
        out_specs=(any_space, any_space),
        scratch_shapes=[
            v((features, columns), BF),
            v((2 * span, features), BF),
            v((2 * span, features), BF),
            v((4 * span, features), BF),
            v((4 * span, features), BF),
            v((4 * span, features), BF),
            v((4 * span, 2 * width), BF),
            v((4 * span, width), BF),
            v((2 * span, features), BF),
            v((2 * span, features), BF),
            v((2 * span, features), BF),
            v((span, features), BF),
            v((span, width), BF),
            v((span, features), F32),
            v((span, features), BF),
            v((span, features), BF),
            v((pairs, CHUNK, columns), BF),
            v((pairs, CHUNK, columns), BF),
            v((CHUNK, columns), F32),
            v((sums, CHUNK, columns), BF),
            v((sums, CHUNK, columns), BF),
            v((shard, columns), F32),
            dma((11,)),
            dma((groups, 2)),
            dma((groups, 2)),
            dma((groups, 2)),
            dma((groups, 2)),
            dma((5,)),
            dma((5,)),
            dma((4,)),
            dma((4,)),
            dma((pairs,)),
            dma((pairs,)),
            dma((sums,)),
            dma((sums,)),
            dma((4,)),
            dma((2,)),
            pltpu.SemaphoreType.REGULAR,
            pltpu.SemaphoreType.REGULAR,
        ],
        compiler_params=pltpu.CompilerParams(
            collective_id=0, has_side_effects=True, vmem_limit_bytes=60 * 2**20
        ),
    )(x, inc, cot, obj, kept, w)
    return hand_out(*results)


def hand_out(out, grads):
    steps = 8
    rows = grads.shape[1] // steps
    count = steps + out.shape[0]

    def body(out_ref, grads_ref, out_to, grads_to, out_mid, grads_mid, sem_in, sem_out):
        parts = [(grads_ref, grads_mid, grads_to, (0, pl.ds(i * rows, rows))) for i in range(steps)]
        parts += [(out_ref, out_mid, out_to, (i,)) for i in range(out.shape[0])]
        taken = [pltpu.make_async_copy(a.at[at], b.at[at], sem_in.at[i]) for i, (a, b, _, at) in enumerate(parts)]
        given = [pltpu.make_async_copy(b.at[at], c.at[at], sem_out.at[i]) for i, (_, b, c, at) in enumerate(parts)]
        for copy in taken:
            copy.start()
        for one, two in zip(taken, given):
            one.wait()
            two.start()
        for copy in given:
            copy.wait()

    any_space = pl.BlockSpec(memory_space=pl.ANY)
    return pl.pallas_call(
        body,
        out_shape=(
            jax.ShapeDtypeStruct(out.shape, out.dtype),
            jax.ShapeDtypeStruct(grads.shape, grads.dtype),
        ),
        in_specs=[any_space] * 2,
        out_specs=(any_space, any_space),
        scratch_shapes=[
            pltpu.VMEM(out.shape, out.dtype),
            pltpu.VMEM(grads.shape, grads.dtype),
            pltpu.SemaphoreType.DMA((count,)),
            pltpu.SemaphoreType.DMA((count,)),
        ],
    )(out, grads)


def solution(mesh):
    in_specs = (
        P(None, "dp", "section", None),
        P(None, "dp", None, None),
        P(None, "dp", "section", None),
        P(None, "dp", None, None),
        P(None, None, "dp", "section", None),
        P("section", "dp", None),
    )
    out_specs = (P(None, "dp", "section", None), P("section", "dp", None))
    body = functools.partial(on_device, mesh.shape["section"], mesh.shape["dp"])
    return jax.shard_map(body, mesh=mesh, in_specs=in_specs, out_specs=out_specs, check_vma=False)
```
